32 devices in a mesh: groups: 2 (over y), ens: 4 (over z), amp: 4 (over x, core).
Axes of the slice: x: 2, y: 2, z: 4, core: 2. Of those that a mesh axis runs over, the one named last changes fastest.
Arguments:
- states: bfloat16 [64, 2, 262144], P(('groups', 'ens'), None, 'amp'), parts along dimension 0, may hold values from -6 to 6
- layer_angles: int32 [64, 16, 7, 2], P(('groups', 'ens')), parts along dimension 0, may hold values from 0 to 63
- entangler: int32 [64, 16, 6], P(('groups', 'ens')), parts along dimension 0, may hold values 0 or 1
- global_angles: int32 [64, 2], P(('groups', 'ens')), parts along dimension 0, may hold values from 0 to 63
Outputs:
- correlations: float32 [2, 64, 32], P(None, ('groups', 'ens'), 'amp'), parts along dimension 1
The draws below stay inside these ranges and needn't reach their ends.
There are 2 independent parts, one for each index of `groups`. The reference program is written for one: setup_inputs(seed, part) draws one part's arguments, and reference() takes and returns one part's arrays. A program takes and returns all parts, laid end to end along the dimension named above; each array names one. Nothing has to cross between parts.
All inputs are finite; a program needn't handle non-finite values. No bound on the sum of `entangler` on one device may be relied on, other than what follows from the above.
Results may differ from the reference program's by a relative error of at most 0.035.
Values may be sent and summed in bfloat16 or wider, within the bound.
A program may use at most 64 MiB of HBM per device.

```python
import math
import jax
import jax.numpy as jnp
from jax import lax

JOINED = 7
LAYERS = 16
TABLE = 64
CIRC = 32
AMPS = 262144


def place_ends(entries, rng, smallest, high):
    shape = entries.shape
    place = [jax.random.randint(jax.random.fold_in(rng, axis), (), 0, shape[axis]) for axis in range(len(shape))]
    entries = entries.at[tuple(place)].set(smallest)
    longest = shape.index(max(shape))
    place[longest] = (place[longest] + 1) % shape[longest]
    return entries.at[tuple(place)].set(high)


def steps_of(rng, shape, shards, least, top_value):
    factor_of = 1.0
    for position, parts in shards:
        heights = jax.random.uniform(jax.random.fold_in(jax.random.fold_in(rng, 6), position), (parts,), jnp.float32, least / len(shards), top_value / len(shards))
        factor_of = factor_of * jnp.repeat(jnp.exp(heights), shape[position] // parts).reshape((-1,) + (1,) * (len(shape) - 1 - position))
    return factor_of


def noise(stream_key, extent, spread, reach, shards=(), kind=jnp.bfloat16):
    values = jax.random.normal(stream_key, extent, jnp.float32) * spread
    if len(shards) > 0:
        values = steps_of(stream_key, extent, shards, -0.22, 0.18) * values
    return jnp.clip(values, min=-reach, max=reach).astype(kind)


def setup_inputs(seed: int = 0, part: int = 0) -> dict:
    seeds = jax.random.split(jax.random.key(seed), 5)
    part_splits = jax.random.split(jax.random.fold_in(seeds[4], part), 5)
    return {
        "states": noise(part_splits[0], (CIRC, 2, AMPS), 1.0, 6.0, ((0, 4), (2, 4))),
        "layer_angles": place_ends(jax.random.randint(part_splits[1], (CIRC, LAYERS, JOINED, 2), 0, TABLE), jax.random.fold_in(part_splits[1], 1), 0, TABLE - 1).astype(jnp.int32),
        "entangler": place_ends((jax.random.randint(part_splits[2], (CIRC, LAYERS, JOINED - 1), 0, 2) < 1).astype(jnp.int32), jax.random.fold_in(part_splits[2], 1), 0, 1),
        "global_angles": place_ends(jax.random.randint(part_splits[3], (CIRC, 2), 0, TABLE), jax.random.fold_in(part_splits[3], 1), 0, TABLE - 1).astype(jnp.int32),
    }


def rotation(polar_index, azimuth_index):
    polar = polar_index.astype(jnp.float32) * (math.pi / TABLE)
    azimuth = azimuth_index.astype(jnp.float32) * (math.pi / TABLE)
    cos_polar = jnp.cos(polar)
    sin_polar = jnp.sin(polar)
    cos_azim = jnp.cos(azimuth)
    sin_azim = jnp.sin(azimuth)
    return ((cos_azim * cos_polar, -sin_azim * cos_polar), (-cos_azim * sin_polar, sin_azim * sin_polar), (cos_azim * sin_polar, sin_azim * sin_polar), (cos_azim * cos_polar, sin_azim * cos_polar))

def pick_entry(gate, which, out_bit, in_bit):
    first = gate[0][which][:, None, None]
    second = gate[1][which][:, None, None]
    third = gate[2][which][:, None, None]
    fourth = gate[3][which][:, None, None]
    return jnp.where(out_bit == 0, jnp.where(in_bit == 0, first, second), jnp.where(in_bit == 0, third, fourth))

def layer_weights(angles, links):
    order = 2 ** JOINED
    circuits = angles.shape[0]
    index_row = jnp.arange(order, dtype=jnp.int32)
    real_part = jnp.ones((circuits, order, order), jnp.float32)
    imag_part = jnp.zeros((circuits, order, order), jnp.float32)
    for qubit_index in range(JOINED):
        gate = rotation(angles[:, qubit_index, 0], angles[:, qubit_index, 1])
        bit_row = index_row // 2 ** qubit_index % 2
        out_bit = bit_row[None, :, None]
        in_bit = bit_row[None, None, :]
        factor_real = pick_entry(gate, 0, out_bit, in_bit)
        factor_imag = pick_entry(gate, 1, out_bit, in_bit)
        real_part, imag_part = (real_part * factor_real - imag_part * factor_imag, real_part * factor_imag + imag_part * factor_real)
    sign_flip = jnp.ones((circuits, order), jnp.float32)
    for qubit_index in range(JOINED - 1):
        both_set = index_row // 2 ** qubit_index % 2 * (index_row // 2 ** (qubit_index + 1) % 2)
        flipped = links[:, qubit_index][:, None] * both_set[None, :]
        sign_flip = sign_flip * (1.0 - 2.0 * flipped.astype(jnp.float32))
    real_part = real_part * sign_flip[:, :, None]
    imag_part = imag_part * sign_flip[:, :, None]
    real_turned = jnp.transpose(real_part, (0, 2, 1))
    imag_turned = jnp.transpose(imag_part, (0, 2, 1))
    top_row = jnp.stack([real_turned, imag_turned], 1)
    bottom_row = jnp.stack([-imag_turned, real_turned], 1)
    return jnp.stack([top_row, bottom_row], 1).astype(jnp.bfloat16)

def bridge_signs(local):
    index_all = jnp.arange(local, dtype=jnp.int32)
    both_set = index_all // 2 ** (JOINED - 1) % 2 * (index_all // 2 ** JOINED % 2)
    return 1.0 - 2.0 * both_set.astype(jnp.float32)

def apply_layer(current, weights, upper_block):
    circuits, _, local = current.shape
    order = weights.shape[-1]
    matrices = weights.astype(jnp.float32)
    if upper_block:
        reshaped = current.astype(jnp.float32).reshape(circuits, 2, local // (order * order), order, order)
        result = jnp.einsum('cphnl,cpqnm->cqhml', reshaped, matrices, precision=lax.Precision.HIGHEST)
    else:
        reshaped = current.astype(jnp.float32).reshape(circuits, 2, local // order, order)
        result = jnp.einsum('cprn,cpqnm->cqrm', reshaped, matrices, precision=lax.Precision.HIGHEST)
    result = result.reshape(circuits, 2, local) * bridge_signs(local)[None, None, :]
    return result.astype(jnp.bfloat16)

def scaled(coefficient, amplitudes):
    real_c = coefficient[0][:, None]
    imag_c = coefficient[1][:, None]
    return jnp.stack([real_c * amplitudes[:, 0] - imag_c * amplitudes[:, 1], real_c * amplitudes[:, 1] + imag_c * amplitudes[:, 0]], 1)

def reference(states, layer_angles, entangler, global_angles):
    current = states
    for layer in range(LAYERS):
        weights = layer_weights(layer_angles[:, layer], entangler[:, layer])
        current = apply_layer(current, weights, layer % 2 == 1)
    halfway = AMPS // 2
    lower_amps = current[:, :, :halfway].astype(jnp.float32)
    upper_amps = current[:, :, halfway:].astype(jnp.float32)
    gate = rotation(global_angles[:, 0], global_angles[:, 1])
    new_lower = scaled(gate[0], lower_amps) + scaled(gate[1], upper_amps)
    new_upper = scaled(gate[2], lower_amps) + scaled(gate[3], upper_amps)
    final_states = jnp.concatenate([new_lower, new_upper], 2).astype(jnp.bfloat16)
    real_amps = final_states[:, 0]
    imag_amps = final_states[:, 1]
    gram_real = jnp.dot(real_amps, real_amps.T, preferred_element_type=jnp.float32) + jnp.dot(imag_amps, imag_amps.T, preferred_element_type=jnp.float32)
    gram_imag = jnp.dot(real_amps, imag_amps.T, preferred_element_type=jnp.float32) - jnp.dot(imag_amps, real_amps.T, preferred_element_type=jnp.float32)
    circuit_row = jnp.arange(CIRC, dtype=jnp.int32)
    off_diagonal = jnp.where(circuit_row[:, None] == circuit_row[None, :], 0.0, 1.0).astype(jnp.float32)
    factor = off_diagonal / math.sqrt(AMPS)
    return jnp.stack([gram_real * factor, gram_imag * factor])
```

```python
import functools
import math

import jax
import jax.numpy as jnp
import numpy as np
from jax import lax
from jax.experimental import pallas as pl
from jax.experimental.pallas import tpu as pltpu
from jax.sharding import PartitionSpec as P

JOINED = 7
TABLE = 64
ORDER = 2**JOINED
LOW = 3
MESH_ID = pl.DeviceIdType.MESH


def from_partner(array, axis, bit):
    return lax.ppermute(array, axis, [(i, i ^ 1 << bit) for i in range(lax.axis_size(axis))])


def rotation(polar_index, azimuth_index):
    polar = polar_index.astype(jnp.float32) * (math.pi / TABLE)
    azimuth = azimuth_index.astype(jnp.float32) * (math.pi / TABLE)
    cos_polar = jnp.cos(polar)
    sin_polar = jnp.sin(polar)
    cos_azim = jnp.cos(azimuth)
    sin_azim = jnp.sin(azimuth)
    return (
        (cos_azim * cos_polar, -sin_azim * cos_polar),
        (-cos_azim * sin_polar, sin_azim * sin_polar),
        (cos_azim * sin_polar, sin_azim * sin_polar),
        (cos_azim * cos_polar, sin_azim * cos_polar),
    )


def bit_of(shape, dim, bit, shift=0):
    return (lax.broadcasted_iota(jnp.int32, shape, dim) >> (bit - shift)) & 1


class Tables:
    def __init__(self, circuits, table_ref, angle_ref, link_ref):
        self.circuits, self.table, self.angle, self.link = circuits, table_ref, angle_ref, link_ref

    def cos_sin(self, circuit, layer, k, which):
        index = self.angle[(circuit * JOINED + k) * 2 + which, layer]
        return self.table[index], self.table[index + TABLE]

    def flip(self, circuit, layer, k):
        return 1.0 - 2.0 * self.link[k * self.circuits + circuit, layer].astype(jnp.float32)


def part_factor(tables, circuit, layer, upper, high):
    qubits = range(LOW, JOINED) if high else range(LOW)
    shape = (2 ** len(qubits), ORDER)
    shift = LOW if high else 0
    row = {k: bit_of(shape, 0, k, shift) for k in qubits}
    lane = {k: bit_of(shape, 1, k) for k in range(JOINED)}
    out = row if upper else lane
    real = imag = None
    turn = None
    for k in qubits:
        cos_t, sin_t = tables.cos_sin(circuit, layer, k, 0)
        cos_f, sin_f = tables.cos_sin(circuit, layer, k, 1)
        side = (2 * out[k] - 1).astype(jnp.float32)
        factor = jnp.where(row[k] == lane[k], cos_t, side * sin_t)
        turn = factor if turn is None else turn * factor
        step = side * sin_f
        if real is None:
            real, imag = jnp.full(shape, cos_f), step
        else:
            real, imag = real * cos_f - imag * step, real * step + imag * cos_f
    for k in range(JOINED - 1):
        inside = k in qubits and k + 1 in qubits
        if inside or (not upper and not high and k == LOW - 1):
            turn = jnp.where(out[k] * out[k + 1] == 1, tables.flip(circuit, layer, k) * turn, turn)
    return real * turn, imag * turn


def build(tables, circuit, layer, upper, w_ref):
    low_real, low_imag = part_factor(tables, circuit, layer, upper, False)
    high_real, high_imag = part_factor(tables, circuit, layer, upper, True)
    lows = [(low_real, low_imag)] * 2
    if upper:
        crossed = bit_of(low_real.shape, 0, LOW - 1) == 1
        flip = tables.flip(circuit, layer, LOW - 1)
        lows[1] = tuple(jnp.where(crossed, flip * v, v) for v in lows[0])
    for pair in range(ORDER // 16):
        reals, imags = [], []
        for odd in range(2):
            r = 2 * pair + odd
            a_real = jnp.broadcast_to(high_real[r : r + 1], (8, ORDER))
            a_imag = jnp.broadcast_to(high_imag[r : r + 1], (8, ORDER))
            b_real, b_imag = lows[odd]
            reals.append(a_real * b_real - a_imag * b_imag)
            imags.append(a_real * b_imag + a_imag * b_real)
        real = jnp.concatenate(reals, 0)
        imag = jnp.concatenate(imags, 0)
        plus, minus = imag.astype(jnp.bfloat16), (-imag).astype(jnp.bfloat16)
        real = real.astype(jnp.bfloat16)
        top, bottom = (minus, plus) if upper else (plus, minus)
        rows = pl.ds(16 * pair, 16)
        rows_below = pl.ds(ORDER + 16 * pair, 16)
        w_ref[rows, :ORDER] = real
        w_ref[rows, ORDER:] = top
        w_ref[rows_below, :ORDER] = bottom
        w_ref[rows_below, ORDER:] = real


def bridge(values):
    rows, columns = values.shape
    shape = (1, 8, columns)
    odd = bit_of(shape, 1, 0) * bit_of(shape, 2, JOINED - 1)
    sign = (1 - 2 * odd).astype(jnp.float32)
    return (values.reshape(rows // 8, 8, columns) * sign).reshape(rows, columns)


def chains_of(blocks):
    return 2 if blocks % 2 == 0 else 1


def run_layers(circuit, layers, tables, x_ref, t_ref, wl_ref, wu_ref, s_ref):
    rows = t_ref.shape[0]
    chains, _, wide = s_ref.shape
    blocks = wide // ORDER

    def spread(step, carry):
        flat = x_ref[:, pl.ds(pl.multiple_of(step * 16 * ORDER, 16 * ORDER), 16 * ORDER)]
        tiles = flat.astype(jnp.float32).reshape(2, 16, ORDER).astype(jnp.bfloat16)
        rows_at = pl.ds(pl.multiple_of(step * 16, 16), 16)
        t_ref[rows_at, :ORDER] = tiles[0]
        t_ref[rows_at, ORDER:] = tiles[1]
        return carry

    lax.fori_loop(0, rows // 16, spread, 0, unroll=4)
    build(tables, circuit, 0, False, wl_ref)

    def two(pair, carry):
        layer = 2 * pair
        following = jnp.minimum(layer + 2, layers - 2)
        for h in range(chains):
            y = jnp.dot(t_ref[h * wide : (h + 1) * wide], wl_ref[...], preferred_element_type=jnp.float32)
            y = bridge(y).astype(jnp.bfloat16)
            for b in range(blocks):
                for p in range(2):
                    s_ref[h, p * ORDER : (p + 1) * ORDER, b * ORDER : (b + 1) * ORDER] = y[
                        b * ORDER : (b + 1) * ORDER, p * ORDER : (p + 1) * ORDER
                    ]
            if h == 0:
                build(tables, circuit, layer + 1, True, wu_ref)
        for h in range(chains):
            y = jnp.dot(wu_ref[...], s_ref[h], preferred_element_type=jnp.float32)
            y = bridge(y).astype(jnp.bfloat16)
            for b in range(blocks):
                for p in range(2):
                    at = h * wide + b * ORDER
                    t_ref[at : at + ORDER, p * ORDER : (p + 1) * ORDER] = y[
                        p * ORDER : (p + 1) * ORDER, b * ORDER : (b + 1) * ORDER
                    ]
            if h == 0:
                build(tables, circuit, following, False, wl_ref)
        return carry

    lax.fori_loop(0, layers // 2, two, 0)


def layers_scratch(rows):
    chains = chains_of(rows // ORDER)
    return [
        pltpu.VMEM((2 * ORDER, 2 * ORDER), jnp.bfloat16),
        pltpu.VMEM((2 * ORDER, 2 * ORDER), jnp.bfloat16),
        pltpu.VMEM((chains, 2 * ORDER, rows // chains), jnp.bfloat16),
    ]


def layers_kernel(circuits, layers, table_ref, angle_ref, link_ref, x_ref, t_ref, wl_ref, wu_ref, s_ref):
    tables = Tables(circuits, table_ref, angle_ref, link_ref)
    run_layers(pl.program_id(0), layers, tables, x_ref.at[0], t_ref.at[0], wl_ref, wu_ref, s_ref)


def small_tables(layer_angles, entangler):
    circuits, layers = layer_angles.shape[:2]
    angle = np.arange(TABLE, dtype=np.float64) * (math.pi / TABLE)
    table = jnp.asarray(np.concatenate([np.cos(angle), np.sin(angle)]).astype(np.float32))
    angles = jnp.transpose(layer_angles, (0, 2, 3, 1)).reshape(circuits * JOINED * 2, layers)
    links = jnp.transpose(entangler, (2, 0, 1)).reshape((JOINED - 1) * circuits, layers)
    return table, angles, links


def all_layers(states, layer_angles, entangler):
    circuits, _, local = states.shape
    rows = local // ORDER
    layers = layer_angles.shape[1]
    smem = pl.BlockSpec(memory_space=pltpu.SMEM)
    return pl.pallas_call(
        functools.partial(layers_kernel, circuits, layers),
        grid=(circuits,),
        out_shape=jax.ShapeDtypeStruct((circuits, rows, 2 * ORDER), jnp.bfloat16),
        in_specs=[smem, smem, smem, pl.BlockSpec((1, 2, local), lambda g: (g, 0, 0))],
        out_specs=pl.BlockSpec((1, rows, 2 * ORDER), lambda g: (g, 0, 0)),
        scratch_shapes=layers_scratch(rows),
        compiler_params=pltpu.CompilerParams(vmem_limit_bytes=32 << 20),
    )(*small_tables(layer_angles, entangler), states)


def gate_pair(gate, low, high):
    outs = []
    for r in range(2):
        a_real, a_imag, b_real, b_imag = (gate[4 * r + k] for k in range(4))
        real = a_real * low[0] - a_imag * low[1] + (b_real * high[0] - b_imag * high[1])
        imag = a_real * low[1] + a_imag * low[0] + (b_real * high[1] + b_imag * high[0])
        outs.append((real, imag))
    return outs


def exact_dot(values, picks, dims):
    total = None
    for _ in range(3):
        term = values.astype(jnp.bfloat16)
        values = values - term.astype(jnp.float32)
        operands = (term, picks) if dims[0] == "values" else (picks, term)
        part = lax.dot_general(*operands, (dims[1], ((), ())), preferred_element_type=jnp.float32)
        total = part if total is None else total + part
    return total


def fused_kernel(
    layers, ens, amp,
    table_ref, angle_ref, link_ref, global_ref, x_hbm, o_ref,
    wl_ref, wu_ref, s_ref, x_ref, t_ref, r_ref, c_ref, cs_ref, f_ref, h_ref, l_ref, q_ref,
    load_sem, small_sem, send_sem, recv_sem, gate_send, gate_recv, sum_send, sum_recv,
):
    circuits, rows, _ = t_ref.shape
    total = ens * circuits
    share = rows // (2 * ens)
    parts = share // 16
    half = 2 * ORDER // 4
    bit = amp.bit_length() - 2
    me = lax.axis_index("ens")
    here = lax.axis_index("amp")
    side = (here // 2**bit) % 2
    rest = here - side * 2**bit
    tables = Tables(circuits, table_ref, angle_ref, link_ref)

    barrier = pltpu.get_barrier_semaphore()
    everyone = [(k // amp, k % amp) for k in range(1, ens * amp)]
    for e, a in everyone:
        pl.semaphore_signal(
            barrier, inc=1, device_id={"ens": (me + e) % ens, "amp": (here + a) % amp}, device_id_type=MESH_ID
        )

    def load(circuit):
        return pltpu.make_async_copy(x_hbm.at[circuit], x_ref.at[circuit], load_sem.at[circuit])

    for circuit in range(circuits):
        load(circuit).start()

    lane = lax.broadcasted_iota(jnp.int32, (1, ORDER), 1)
    for circuit in range(circuits):
        polar, azimuth = global_ref[0, circuit], global_ref[1, circuit]
        cos_t, sin_t = table_ref[polar], table_ref[polar + TABLE]
        cos_f, sin_f = table_ref[azimuth], table_ref[azimuth + TABLE]
        entries = (
            cos_f * cos_t, -sin_f * cos_t, -cos_f * sin_t, sin_f * sin_t,
            cos_f * sin_t, sin_f * sin_t, cos_f * cos_t, sin_f * cos_t,
        )
        line = jnp.zeros((1, ORDER), jnp.float32)
        for k, entry in enumerate(entries):
            line = jnp.where(lane == k, entry, line)
        c_ref[pl.ds(me, 1), circuit : circuit + 1] = line[None]

    def gate_copy(k, source):
        return pltpu.make_async_remote_copy(
            src_ref=c_ref.at[source],
            dst_ref=c_ref.at[source],
            send_sem=gate_send.at[k - 1],
            recv_sem=gate_recv.at[k - 1],
            device_id={"ens": (me + k) % ens},
            device_id_type=MESH_ID,
        )

    peers = sorted(((k // ens, k % ens) for k in range(1, 2 * ens)), key=lambda p: (abs(2 * p[1] - ens), p[0]))

    def piece(k, circuit, from_side, from_ens):
        across, along = peers[k]
        to_side = side + across - 2 * side * across
        to_ens = (me + along) % ens
        start = pl.multiple_of((to_side * ens + to_ens) * share, share)
        return pltpu.make_async_remote_copy(
            src_ref=t_ref.at[circuit, pl.ds(start, share)],
            dst_ref=r_ref.at[from_side, from_ens * circuits + circuit],
            send_sem=send_sem.at[circuit, k],
            recv_sem=recv_sem.at[circuit, k],
            device_id={"ens": to_ens, "amp": to_side * 2**bit + rest},
            device_id_type=MESH_ID,
        )

    def compute(circuit, carry):
        load(circuit).wait()
        run_layers(circuit, layers, tables, x_ref.at[circuit], t_ref.at[circuit], wl_ref, wu_ref, s_ref)

        @pl.when(circuit == 0)
        def _():
            pl.semaphore_wait(barrier, len(everyone))
            for k in range(1, ens):
                gate_copy(k, me).start()

        for k in range(len(peers)):
            piece(k, circuit, side, me).start()
        own = pl.multiple_of((side * ens + me) * share, share)
        r_ref[side, me * circuits + circuit] = t_ref[circuit, pl.ds(own, share), :]
        return carry

    lax.fori_loop(0, circuits, compute, 0)
    for k in range(1, ens):
        gate_copy(k, (me + ens - k) % ens).wait_recv()
    scalars = pltpu.make_async_copy(c_ref, cs_ref, small_sem)
    scalars.start()
    f_ref[...] = jnp.zeros_like(f_ref)
    l_ref[...] = jnp.zeros_like(l_ref)
    scalars.wait()

    depth = f_ref.shape[2]

    def gram(circuit, carry):
        for k, (across, along) in enumerate(peers):
            piece(k, circuit, side + across - 2 * side * across, (me + ens - along) % ens).wait_recv()
        for e in range(ens):
            which = e * circuits + circuit
            gate = [cs_ref[e, circuit, k] for k in range(8)]
            low = r_ref[0, which].astype(jnp.float32)
            high = r_ref[1, which].astype(jnp.float32)
            outs = gate_pair(gate, (low[:, :ORDER], low[:, ORDER:]), (high[:, :ORDER], high[:, ORDER:]))
            for x, (real, imag) in enumerate(outs):
                real = real.astype(jnp.bfloat16)
                imag = imag.astype(jnp.bfloat16)
                minus = -real
                for part in range(parts):
                    at = (x * parts + part) * 2 * ORDER
                    take = slice(16 * part, 16 * part + 16)
                    for ref, row in ((f_ref, which), (h_ref, e)):
                        ref[row, :, at : at + ORDER] = real[take]
                        ref[row, :, at + ORDER : at + 2 * ORDER] = imag[take]
                    h_ref[ens + e, :, at : at + ORDER] = imag[take]
                    h_ref[ens + e, :, at + ORDER : at + 2 * ORDER] = minus[take]
        fresh = 2 * ens * 16
        full = lax.dot_general(
            f_ref[...].reshape(total * 16, depth), h_ref[...].reshape(fresh, depth),
            (((1,), (1,)), ((), ())), preferred_element_type=jnp.float32,
        )
        shape = (1, 16, fresh)
        same = lax.broadcasted_iota(jnp.int32, shape, 1) == lax.broadcasted_iota(jnp.int32, shape, 2) % 16
        kept = jnp.where(same, full.reshape(total, 16, fresh), 0.0).sum(1)

        shape = (fresh, ORDER)
        source = lax.broadcasted_iota(jnp.int32, shape, 0) // 16
        target = lax.broadcasted_iota(jnp.int32, shape, 1)
        place = jnp.where(source >= ens, half + (source - ens) * circuits, source * circuits) + circuit
        above = exact_dot(kept, jnp.where(place == target, 1.0, 0.0).astype(jnp.bfloat16), ("values", ((1,), (0,))))

        shape = (half, fresh)
        row = lax.broadcasted_iota(jnp.int32, shape, 0)
        is_imag = lax.broadcasted_iota(jnp.int32, shape, 1) // 16 >= ens
        before = (row % circuits < circuit) & (row < total)
        doubled = kept if total == half else jnp.concatenate([kept, jnp.zeros((half - total, fresh), jnp.float32)], 0)
        stacked = jnp.concatenate(
            [jnp.where(before & ~is_imag, doubled, 0.0), jnp.where(before & is_imag, -doubled, 0.0)], 0
        )
        shape = (total, fresh)
        row = lax.broadcasted_iota(jnp.int32, shape, 0)
        source = lax.broadcasted_iota(jnp.int32, shape, 1) // 16 % ens
        gather = jnp.where(row == source * circuits + circuit, 1.0, 0.0).astype(jnp.bfloat16)
        mirrored = exact_dot(stacked, gather, ("picks", ((1,), (1,))))
        l_ref[...] += above + mirrored
        return carry

    lax.fori_loop(0, circuits, gram, 0)

    def slab(k):
        e, a = everyone[k]
        to = (me + e) % ens
        return pltpu.make_async_remote_copy(
            src_ref=l_ref.at[pl.ds(pl.multiple_of(to * circuits, circuits), circuits)],
            dst_ref=q_ref.at[k],
            send_sem=sum_send.at[k],
            recv_sem=sum_recv.at[k],
            device_id={"ens": to, "amp": (here + a) % amp},
            device_id_type=MESH_ID,
        )

    for k in range(len(everyone)):
        slab(k).start()
    result = l_ref[pl.ds(pl.multiple_of(me * circuits, circuits), circuits)]
    for k in range(len(everyone)):
        slab(k).wait_recv()
        result = result + q_ref[k]
    columns = total // amp
    result = pltpu.roll(result, (2 * half - here * columns) % (2 * half), 1)
    shape = (circuits, columns)
    row = lax.broadcasted_iota(jnp.int32, shape, 0) + me * circuits
    column = lax.broadcasted_iota(jnp.int32, shape, 1) + here * columns
    scale = jnp.where(row == column, 0.0, 1.0 / math.sqrt(rows * ORDER * amp))
    o_ref[0] = result[:, :columns] * scale
    o_ref[1] = result[:, half : half + columns] * scale

    for k in range(len(everyone)):
        slab(k).wait_send()
    for k in range(1, ens):
        gate_copy(k, me).wait_send()

    def drain(circuit, carry):
        for k in range(len(peers)):
            piece(k, circuit, side, me).wait_send()
        return carry

    lax.fori_loop(0, circuits, drain, 0)


def fused(states, layer_angles, entangler, global_angles):
    circuits, _, local = states.shape
    rows = local // ORDER
    layers = layer_angles.shape[1]
    ens, amp = lax.axis_size("ens"), lax.axis_size("amp")
    total = ens * circuits
    share = rows // (2 * ens)
    depth = 2 * (share // 16) * 2 * ORDER
    smem = pl.BlockSpec(memory_space=pltpu.SMEM)
    return pl.pallas_call(
        functools.partial(fused_kernel, layers, ens, amp),
        out_shape=jax.ShapeDtypeStruct((2, circuits, total // amp), jnp.float32),
        in_specs=[smem, smem, smem, smem, pl.BlockSpec(memory_space=pl.ANY)],
        out_specs=pl.BlockSpec(memory_space=pltpu.VMEM),
        scratch_shapes=layers_scratch(rows)
        + [
            pltpu.VMEM((circuits, 2, local), jnp.bfloat16),
            pltpu.VMEM((circuits, rows, 2 * ORDER), jnp.bfloat16),
            pltpu.VMEM((2, total, share, 2 * ORDER), jnp.bfloat16),
            pltpu.VMEM((ens, circuits, ORDER), jnp.float32),
            pltpu.SMEM((ens, circuits, ORDER), jnp.float32),
            pltpu.VMEM((total, 16, depth), jnp.bfloat16),
            pltpu.VMEM((2 * ens, 16, depth), jnp.bfloat16),
            pltpu.VMEM((total, ORDER), jnp.float32),
            pltpu.VMEM((ens * amp - 1, circuits, ORDER), jnp.float32),
            pltpu.SemaphoreType.DMA((circuits,)),
            pltpu.SemaphoreType.DMA,
            pltpu.SemaphoreType.DMA((circuits, 2 * ens - 1)),
            pltpu.SemaphoreType.DMA((circuits, 2 * ens - 1)),
            pltpu.SemaphoreType.DMA((ens - 1,)),
            pltpu.SemaphoreType.DMA((ens - 1,)),
            pltpu.SemaphoreType.DMA((ens * amp - 1,)),
            pltpu.SemaphoreType.DMA((ens * amp - 1,)),
        ],
        compiler_params=pltpu.CompilerParams(
            vmem_limit_bytes=62 << 20, collective_id=0, has_side_effects=True
        ),
    )(*small_tables(layer_angles, entangler), jnp.transpose(global_angles), states)


def finish(summed, states, circuits):
    columns = lax.axis_size("ens") * circuits // lax.axis_size("amp")
    row_index = lax.axis_index("ens") * circuits + jnp.arange(circuits, dtype=jnp.int32)
    column_index = lax.axis_index("amp") * columns + jnp.arange(columns, dtype=jnp.int32)
    off_diagonal = jnp.where(row_index[:, None] == column_index[None, :], 0.0, 1.0).astype(jnp.float32)
    amplitudes = states.shape[2] * lax.axis_size("amp")
    return summed * (off_diagonal / math.sqrt(amplitudes))[None]


def fits(states):
    circuits, _, local = states.shape
    ens, amp = lax.axis_size("ens"), lax.axis_size("amp")
    rows = local // ORDER
    return (
        rows % (2 * ens * 16) == 0 and circuits % 8 == 0 and ens * circuits <= ORDER // 2
        and ens * circuits % amp == 0 and amp >= 2 and local <= 1 << 16 and ens > 1
    )


def scaled(coefficient, amplitudes):
    real_c = coefficient[0][:, None]
    imag_c = coefficient[1][:, None]
    return jnp.stack(
        [
            real_c * amplitudes[:, 0] - imag_c * amplitudes[:, 1],
            real_c * amplitudes[:, 1] + imag_c * amplitudes[:, 0],
        ],
        1,
    )


def choose_pair(upper_side, when_lower, when_upper):
    return (
        jnp.where(upper_side == 0, when_lower[0], when_upper[0]),
        jnp.where(upper_side == 0, when_lower[1], when_upper[1]),
    )


def pair_tile(mine, remote):
    products = jnp.einsum("ipa,jqa->pqij", mine, remote, preferred_element_type=jnp.float32)
    return jnp.stack([products[0, 0] + products[1, 1], products[0, 1] - products[1, 0]])


def body(states, layer_angles, entangler, global_angles):
    circuits = states.shape[0]
    if fits(states):
        return fused(states, layer_angles, entangler, global_angles)
    turned = all_layers(states, layer_angles, entangler).reshape(circuits, -1, 2, ORDER)
    current = jnp.swapaxes(turned, 1, 2).reshape(states.shape)
    swap_bit = lax.axis_size("amp").bit_length() - 2
    upper_side = lax.axis_index("amp") // 2**swap_bit % 2
    gate = rotation(global_angles[:, 0], global_angles[:, 1])
    partner = from_partner(current, "amp", swap_bit)
    coeff_self = choose_pair(upper_side, gate[0], gate[3])
    coeff_other = choose_pair(upper_side, gate[1], gate[2])
    final_states = (
        scaled(coeff_self, current.astype(jnp.float32))
        + scaled(coeff_other, partner.astype(jnp.float32))
    ).astype(jnp.bfloat16)
    partials = pair_tile(final_states, lax.all_gather(final_states, "ens", axis=0, tiled=True))
    summed = lax.psum_scatter(partials, "amp", scatter_dimension=2, tiled=True)
    return finish(summed, states, circuits)


def solution(mesh):
    return jax.shard_map(
        body,
        mesh=mesh,
        in_specs=(
            P(("groups", "ens"), None, "amp"),
            P(("groups", "ens"), None, None, None),
            P(("groups", "ens"), None, None),
            P(("groups", "ens"), None),
        ),
        out_specs=P(None, ("groups", "ens"), "amp"),
        check_vma=False,
    )
```

```python
import functools
import math

import jax
import jax.numpy as jnp
import numpy as np
from jax import lax
from jax.experimental import pallas as pl
from jax.experimental.pallas import tpu as pltpu
from jax.sharding import PartitionSpec as P

JOINED = 7
TABLE = 64
ORDER = 2**JOINED
LOW = 3
MESH_ID = pl.DeviceIdType.MESH


def from_partner(array, axis, bit):
    return lax.ppermute(array, axis, [(i, i ^ 1 << bit) for i in range(lax.axis_size(axis))])


def rotation(polar_index, azimuth_index):
    polar = polar_index.astype(jnp.float32) * (math.pi / TABLE)
    azimuth = azimuth_index.astype(jnp.float32) * (math.pi / TABLE)
    cos_polar = jnp.cos(polar)
    sin_polar = jnp.sin(polar)
    cos_azim = jnp.cos(azimuth)
    sin_azim = jnp.sin(azimuth)
    return (
        (cos_azim * cos_polar, -sin_azim * cos_polar),
        (-cos_azim * sin_polar, sin_azim * sin_polar),
        (cos_azim * sin_polar, sin_azim * sin_polar),
        (cos_azim * cos_polar, sin_azim * cos_polar),
    )


def bit_of(shape, dim, bit, shift=0):
    return (lax.broadcasted_iota(jnp.int32, shape, dim) >> (bit - shift)) & 1


class Indexed:
    def __init__(self, circuits, circuit, table_ref, angle_ref, link_ref):
        self.circuits, self.circuit = circuits, circuit
        self.table, self.angle, self.link = table_ref, angle_ref, link_ref

    def cos_sin(self, layer, k, which):
        index = self.angle[(self.circuit * JOINED + k) * 2 + which, layer]
        return self.table[index], self.table[index + TABLE]

    def flip(self, layer, k):
        return 1.0 - 2.0 * self.link[k * self.circuits + self.circuit, layer].astype(jnp.float32)


class Listed:
    def __init__(self, ref):
        self.ref = ref

    def entry(self, r, layer):
        return self.ref[r // 8, r % 8 * 16 + layer]

    def cos_sin(self, layer, k, which):
        return self.entry(2 * k + which, layer), self.entry(2 * JOINED + 2 * k + which, layer)

    def flip(self, layer, k):
        return self.entry(4 * JOINED + k, layer)


def part_factor(tables, layer, upper, high):
    qubits = range(LOW, JOINED) if high else range(LOW)
    shape = (2 ** len(qubits), ORDER)
    shift = LOW if high else 0
    row = {k: bit_of(shape, 0, k, shift) for k in qubits}
    lane = {k: bit_of(shape, 1, k) for k in range(JOINED)}
    out = row if upper else lane
    real = imag = None
    turn = None
    for k in qubits:
        cos_t, sin_t = tables.cos_sin(layer, k, 0)
        cos_f, sin_f = tables.cos_sin(layer, k, 1)
        side = (2 * out[k] - 1).astype(jnp.float32)
        factor = jnp.where(row[k] == lane[k], cos_t, side * sin_t)
        turn = factor if turn is None else turn * factor
        step = side * sin_f
        if real is None:
            real, imag = jnp.full(shape, cos_f), step
        else:
            real, imag = real * cos_f - imag * step, real * step + imag * cos_f
    for k in range(JOINED - 1):
        inside = k in qubits and k + 1 in qubits
        if inside or (not upper and not high and k == LOW - 1):
            turn = jnp.where(out[k] * out[k + 1] == 1, tables.flip(layer, k) * turn, turn)
    return real * turn, imag * turn


def build(tables, layer, upper, w_ref):
    low_real, low_imag = part_factor(tables, layer, upper, False)
    high_real, high_imag = part_factor(tables, layer, upper, True)
    lows = [(low_real, low_imag)] * 2
    if upper:
        crossed = bit_of(low_real.shape, 0, LOW - 1) == 1
        flip = tables.flip(layer, LOW - 1)
        lows[1] = tuple(jnp.where(crossed, flip * v, v) for v in lows[0])
    for pair in range(ORDER // 16):
        reals, imags = [], []
        for odd in range(2):
            r = 2 * pair + odd
            a_real = jnp.broadcast_to(high_real[r : r + 1], (8, ORDER))
            a_imag = jnp.broadcast_to(high_imag[r : r + 1], (8, ORDER))
            b_real, b_imag = lows[odd]
            reals.append(a_real * b_real - a_imag * b_imag)
            imags.append(a_real * b_imag + a_imag * b_real)
        real = jnp.concatenate(reals, 0)
        imag = jnp.concatenate(imags, 0)
        plus, minus = imag.astype(jnp.bfloat16), (-imag).astype(jnp.bfloat16)
        real = real.astype(jnp.bfloat16)
        top, bottom = (minus, plus) if upper else (plus, minus)
        rows = pl.ds(16 * pair, 16)
        rows_below = pl.ds(ORDER + 16 * pair, 16)
        w_ref[rows, :ORDER] = real
        w_ref[rows, ORDER:] = top
        w_ref[rows_below, :ORDER] = bottom
        w_ref[rows_below, ORDER:] = real


def bridge(values):
    rows, columns = values.shape
    shape = (1, 8, columns)
    odd = bit_of(shape, 1, 0) * bit_of(shape, 2, JOINED - 1)
    sign = (1 - 2 * odd).astype(jnp.float32)
    return (values.reshape(rows // 8, 8, columns) * sign).reshape(rows, columns)


def spread(x_ref, t_ref):
    def some(step, carry):
        flat = x_ref[:, pl.ds(pl.multiple_of(step * 16 * ORDER, 16 * ORDER), 16 * ORDER)]
        tiles = flat.astype(jnp.float32).reshape(2, 16, ORDER).astype(jnp.bfloat16)
        rows_at = pl.ds(pl.multiple_of(step * 16, 16), 16)
        t_ref[rows_at, :ORDER] = tiles[0]
        t_ref[rows_at, ORDER:] = tiles[1]
        return carry

    lax.fori_loop(0, t_ref.shape[0] // 16, some, 0, unroll=4)


def run_layers(layers, chains):
    for tables, _, wl_ref, _, _ in chains:
        build(tables, 0, False, wl_ref)

    def two(pair, carry):
        layer = 2 * pair
        following = jnp.minimum(layer + 2, layers - 2)
        for tables, t_ref, wl_ref, wu_ref, s_ref in chains:
            y = jnp.dot(t_ref[...], wl_ref[...], preferred_element_type=jnp.float32)
            y = bridge(y).astype(jnp.bfloat16)
            for b in range(t_ref.shape[0] // ORDER):
                for p in range(2):
                    s_ref[p * ORDER : (p + 1) * ORDER, b * ORDER : (b + 1) * ORDER] = y[
                        b * ORDER : (b + 1) * ORDER, p * ORDER : (p + 1) * ORDER
                    ]
            build(tables, layer + 1, True, wu_ref)
        for tables, t_ref, wl_ref, wu_ref, s_ref in chains:
            y = jnp.dot(wu_ref[...], s_ref[...], preferred_element_type=jnp.float32)
            y = bridge(y).astype(jnp.bfloat16)
            for b in range(t_ref.shape[0] // ORDER):
                for p in range(2):
                    t_ref[b * ORDER : (b + 1) * ORDER, p * ORDER : (p + 1) * ORDER] = y[
                        p * ORDER : (p + 1) * ORDER, b * ORDER : (b + 1) * ORDER
                    ]
            build(tables, following, False, wl_ref)
        return carry

    lax.fori_loop(0, layers // 2, two, 0)


def layers_kernel(circuits, layers, table_ref, angle_ref, link_ref, x_ref, t_ref, wl_ref, wu_ref, s_ref):
    tables = Indexed(circuits, pl.program_id(0), table_ref, angle_ref, link_ref)
    spread(x_ref.at[0], t_ref.at[0])
    run_layers(layers, [(tables, t_ref.at[0], wl_ref, wu_ref, s_ref)])


def small_tables(layer_angles, entangler):
    circuits, layers = layer_angles.shape[:2]
    angle = np.arange(TABLE, dtype=np.float64) * (math.pi / TABLE)
    table = jnp.asarray(np.concatenate([np.cos(angle), np.sin(angle)]).astype(np.float32))
    angles = jnp.transpose(layer_angles, (0, 2, 3, 1)).reshape(circuits * JOINED * 2, layers)
    links = jnp.transpose(entangler, (2, 0, 1)).reshape((JOINED - 1) * circuits, layers)
    return table, angles, links


def all_layers(states, layer_angles, entangler):
    circuits, _, local = states.shape
    rows = local // ORDER
    layers = layer_angles.shape[1]
    smem = pl.BlockSpec(memory_space=pltpu.SMEM)
    return pl.pallas_call(
        functools.partial(layers_kernel, circuits, layers),
        grid=(circuits,),
        out_shape=jax.ShapeDtypeStruct((circuits, rows, 2 * ORDER), jnp.bfloat16),
        in_specs=[smem, smem, smem, pl.BlockSpec((1, 2, local), lambda g: (g, 0, 0))],
        out_specs=pl.BlockSpec((1, rows, 2 * ORDER), lambda g: (g, 0, 0)),
        scratch_shapes=[
            pltpu.VMEM((2 * ORDER, 2 * ORDER), jnp.bfloat16),
            pltpu.VMEM((2 * ORDER, 2 * ORDER), jnp.bfloat16),
            pltpu.VMEM((2 * ORDER, rows), jnp.bfloat16),
        ],
        compiler_params=pltpu.CompilerParams(vmem_limit_bytes=32 << 20),
    )(*small_tables(layer_angles, entangler), states)


def gate_pair(gate, low, high):
    outs = []
    for r in range(2):
        a_real, a_imag, b_real, b_imag = (gate[4 * r + k] for k in range(4))
        real = a_real * low[0] - a_imag * low[1] + (b_real * high[0] - b_imag * high[1])
        imag = a_real * low[1] + a_imag * low[0] + (b_real * high[1] + b_imag * high[0])
        outs.append((real, imag))
    return outs


def exact_dot(values, picks, dims):
    total = None
    for _ in range(3):
        term = values.astype(jnp.bfloat16)
        values = values - term.astype(jnp.float32)
        operands = (term, picks) if dims[0] == "values" else (picks, term)
        part = lax.dot_general(*operands, (dims[1], ((), ())), preferred_element_type=jnp.float32)
        total = part if total is None else total + part
    return total


def listed(angles, links):
    angle = angles.astype(jnp.float32) * (math.pi / TABLE)
    layers = angle.shape[1]
    flips = 1.0 - 2.0 * links.astype(jnp.float32)
    unused = jnp.zeros((64 - 4 * JOINED - (JOINED - 1), layers), jnp.float32)
    values = jnp.concatenate([jnp.cos(angle), jnp.sin(angle), flips, unused], 0)
    shape = (layers, ORDER)
    source = lax.broadcasted_iota(jnp.int32, shape, 0)
    again = jnp.where(source == lax.broadcasted_iota(jnp.int32, shape, 1) % layers, 1.0, 0.0).astype(jnp.bfloat16)
    repeated = exact_dot(values, again, ("values", ((1,), (0,)))).reshape(8, 8, ORDER)
    shape = (1, 8, ORDER)
    mine = lax.broadcasted_iota(jnp.int32, shape, 1) == lax.broadcasted_iota(jnp.int32, shape, 2) // layers
    return jnp.where(mine, repeated, 0.0).sum(1)


GATE_ROW = 7


def fused_kernel(
    layers, ens, amp,
    table_hbm, angle_hbm, link_hbm, global_hbm, x_hbm, o_ref,
    wl_ref, wu_ref, s_ref, x_ref, t_ref, first_x, first_t, r_ref, c_ref, cs_ref, f_ref, h_ref, l_ref, q_ref,
    table_ref, angle_ref, link_ref, global_ref, angle_vmem, link_vmem,
    load_sem, small_sem, send_sem, recv_sem, first_send, first_recv, half_send, half_recv,
    gate_send, gate_recv, sum_send, sum_recv,
):
    circuits, rows, _ = t_ref.shape
    total = ens * circuits
    share = rows // (2 * ens)
    parts = share // 16
    half = 2 * ORDER // 4
    bit = amp.bit_length() - 2
    me = lax.axis_index("ens")
    here = lax.axis_index("amp")
    side = (here // 2**bit) % 2
    rest = here - side * 2**bit
    square = ORDER * ORDER

    barrier = pltpu.get_barrier_semaphore()
    everyone = [(k // amp, k % amp) for k in range(1, ens * amp)]
    everyone = sorted(everyone, key=lambda p: (abs(2 * p[0] - ens), -p[1]))
    for e, a in everyone:
        pl.semaphore_signal(
            barrier, inc=1, device_id={"ens": (me + e) % ens, "amp": (here + a) % amp}, device_id_type=MESH_ID
        )

    def load(circuit):
        return pltpu.make_async_copy(x_hbm.at[circuit], x_ref.at[circuit - 1], load_sem.at[circuit])

    def block(index):
        return x_hbm.at[0, :, pl.ds(pl.multiple_of(index * square, square), square)]

    own_block = pltpu.make_async_copy(block(me), first_x.at[me], load_sem.at[0])
    smalls = [
        pltpu.make_async_copy(source, target, small_sem.at[i])
        for i, (source, target) in enumerate(
            (
                (table_hbm, table_ref), (angle_hbm, angle_ref), (link_hbm, link_ref), (global_hbm, global_ref),
                (angle_hbm, angle_vmem), (link_hbm, link_vmem),
            )
        )
    ]
    for copy in smalls:
        copy.start()
    for circuit in range(1, circuits):
        load(circuit).start()
    own_block.start()

    def first_block(k, source):
        to = (me + k) % ens
        return pltpu.make_async_remote_copy(
            src_ref=block(to),
            dst_ref=first_x.at[source],
            send_sem=first_send.at[k - 1],
            recv_sem=first_recv.at[k - 1],
            device_id={"ens": to},
            device_id_type=MESH_ID,
        )

    far_first = sorted(range(1, ens), key=lambda k: abs(2 * k - ens))
    pl.semaphore_wait(barrier, len(everyone))
    for k in far_first:
        first_block(k, me).start()

    for copy in smalls:
        copy.wait()
    links = jnp.concatenate([link_vmem[k * circuits : k * circuits + 1] for k in range(JOINED - 1)], 0)
    tile = listed(angle_vmem[: 2 * JOINED], links)
    lane = lax.broadcasted_iota(jnp.int32, (1, ORDER), 1)
    line = jnp.zeros((1, ORDER), jnp.float32)
    for circuit in range(circuits):
        polar, azimuth = global_ref[0, circuit], global_ref[1, circuit]
        cos_t, sin_t = table_ref[polar], table_ref[polar + TABLE]
        cos_f, sin_f = table_ref[azimuth], table_ref[azimuth + TABLE]
        entries = (
            cos_f * cos_t, -sin_f * cos_t, -cos_f * sin_t, sin_f * sin_t,
            cos_f * sin_t, sin_f * sin_t, cos_f * cos_t, sin_f * cos_t,
        )
        for k, entry in enumerate(entries):
            line = jnp.where(lane == circuit * 8 + k, entry, line)
    is_gate = lax.broadcasted_iota(jnp.int32, (8, ORDER), 0) == GATE_ROW
    c_ref[pl.ds(me, 1)] = jnp.where(is_gate, line, tile)[None]

    def gate_copy(k, source):
        return pltpu.make_async_remote_copy(
            src_ref=c_ref.at[source],
            dst_ref=c_ref.at[source],
            send_sem=gate_send.at[k - 1],
            recv_sem=gate_recv.at[k - 1],
            device_id={"ens": (me + k) % ens},
            device_id_type=MESH_ID,
        )

    for k in far_first:
        gate_copy(k, me).start()

    peers = sorted(((k // ens, k % ens) for k in range(1, 2 * ens)), key=lambda p: (abs(2 * p[1] - ens), p[0]))

    def piece(k, circuit, from_side, from_ens):
        across, along = peers[k]
        to_side = side + across - 2 * side * across
        to_ens = (me + along) % ens
        start = pl.multiple_of((2 * to_ens + to_side) * share, share)
        return pltpu.make_async_remote_copy(
            src_ref=t_ref.at[circuit, pl.ds(start, share)],
            dst_ref=r_ref.at[from_side, from_ens * circuits + circuit],
            send_sem=send_sem.at[circuit, k],
            recv_sem=recv_sem.at[circuit, k],
            device_id={"ens": to_ens, "amp": to_side * 2**bit + rest},
            device_id_type=MESH_ID,
        )

    def half_copy(e, from_side):
        to_side = 1 - side
        return pltpu.make_async_remote_copy(
            src_ref=first_t.at[e, pl.ds(pl.multiple_of(to_side * share, share), share)],
            dst_ref=r_ref.at[from_side, e * circuits],
            send_sem=half_send.at[e],
            recv_sem=half_recv.at[e],
            device_id={"amp": to_side * 2**bit + rest},
            device_id_type=MESH_ID,
        )

    def chain(circuit, i):
        load(circuit).wait()
        spread(x_ref.at[circuit - 1], t_ref.at[circuit])
        tables = Indexed(circuits, circuit, table_ref, angle_ref, link_ref)
        return tables, t_ref.at[circuit], wl_ref.at[i], wu_ref.at[i], s_ref.at[i]

    def send(circuit):
        for k in range(len(peers)):
            piece(k, circuit, side, me).start()
        own = pl.multiple_of((2 * me + side) * share, share)
        r_ref[side, me * circuits + circuit] = t_ref[circuit, pl.ds(own, share), :]

    def compute(pair, carry):
        both = (2 * pair + 1, 2 * pair + 2)
        run_layers(layers, [chain(circuit, i) for i, circuit in enumerate(both)])
        for circuit in both:
            send(circuit)
        return carry

    lax.fori_loop(0, circuits // 2 - 1, compute, 0)

    for k in range(1, ens):
        gate_copy(k, (me + ens - k) % ens).wait_recv()
    scalars = pltpu.make_async_copy(c_ref, cs_ref, small_sem.at[0])
    scalars.start()
    own_block.wait()
    for k in range(1, ens):
        first_block(k, (me + ens - k) % ens).wait_recv()
    for e in range(ens):
        spread(first_x.at[e], first_t.at[e])
    scalars.wait()
    last = circuits - 1
    run_layers(
        layers,
        [chain(last, 0)]
        + [
            (
                Listed(cs_ref.at[e]), first_t.at[e], wl_ref.at[1 + e], wu_ref.at[1 + e],
                s_ref.at[1, :, e * ORDER : (e + 1) * ORDER],
            )
            for e in range(ens)
        ],
    )
    send(last)
    for e in range(ens):
        half_copy(e, side).start()
        r_ref[side, e * circuits] = first_t[e, pl.ds(pl.multiple_of(side * share, share), share), :]

    f_ref[...] = jnp.zeros_like(f_ref)
    l_ref[...] = jnp.zeros_like(l_ref)

    depth = f_ref.shape[2]

    def gram(circuit, carry):
        @pl.when(circuit == 0)
        def _():
            for e in range(ens):
                half_copy(e, 1 - side).wait_recv()

        @pl.when(circuit != 0)
        def _():
            for k, (across, along) in enumerate(peers):
                piece(k, circuit, side + across - 2 * side * across, (me + ens - along) % ens).wait_recv()

        for e in range(ens):
            which = e * circuits + circuit
            gate = [cs_ref[e, GATE_ROW, circuit * 8 + k] for k in range(8)]
            low = r_ref[0, which].astype(jnp.float32)
            high = r_ref[1, which].astype(jnp.float32)
            outs = gate_pair(gate, (low[:, :ORDER], low[:, ORDER:]), (high[:, :ORDER], high[:, ORDER:]))
            for x, (real, imag) in enumerate(outs):
                real = real.astype(jnp.bfloat16)
                imag = imag.astype(jnp.bfloat16)
                minus = -real
                for part in range(parts):
                    at = (x * parts + part) * 2 * ORDER
                    take = slice(16 * part, 16 * part + 16)
                    for ref, row in ((f_ref, which), (h_ref, e)):
                        ref[row, :, at : at + ORDER] = real[take]
                        ref[row, :, at + ORDER : at + 2 * ORDER] = imag[take]
                    h_ref[ens + e, :, at : at + ORDER] = imag[take]
                    h_ref[ens + e, :, at + ORDER : at + 2 * ORDER] = minus[take]
        fresh = 2 * ens * 16
        full = lax.dot_general(
            f_ref[...].reshape(total * 16, depth), h_ref[...].reshape(fresh, depth),
            (((1,), (1,)), ((), ())), preferred_element_type=jnp.float32,
        )
        shape = (1, 16, fresh)
        same = lax.broadcasted_iota(jnp.int32, shape, 1) == lax.broadcasted_iota(jnp.int32, shape, 2) % 16
        kept = jnp.where(same, full.reshape(total, 16, fresh), 0.0).sum(1)

        shape = (fresh, ORDER)
        source = lax.broadcasted_iota(jnp.int32, shape, 0) // 16
        target = lax.broadcasted_iota(jnp.int32, shape, 1)
        place = jnp.where(source >= ens, half + (source - ens) * circuits, source * circuits) + circuit
        above = exact_dot(kept, jnp.where(place == target, 1.0, 0.0).astype(jnp.bfloat16), ("values", ((1,), (0,))))

        shape = (half, fresh)
        row = lax.broadcasted_iota(jnp.int32, shape, 0)
        is_imag = lax.broadcasted_iota(jnp.int32, shape, 1) // 16 >= ens
        before = (row % circuits < circuit) & (row < total)
        doubled = kept if total == half else jnp.concatenate([kept, jnp.zeros((half - total, fresh), jnp.float32)], 0)
        stacked = jnp.concatenate(
            [jnp.where(before & ~is_imag, doubled, 0.0), jnp.where(before & is_imag, -doubled, 0.0)], 0
        )
        shape = (total, fresh)
        row = lax.broadcasted_iota(jnp.int32, shape, 0)
        source = lax.broadcasted_iota(jnp.int32, shape, 1) // 16 % ens
        gather = jnp.where(row == source * circuits + circuit, 1.0, 0.0).astype(jnp.bfloat16)
        mirrored = exact_dot(stacked, gather, ("picks", ((1,), (1,))))
        l_ref[...] += above + mirrored
        return carry

    lax.fori_loop(0, circuits, gram, 0)

    def slab(k):
        e, a = everyone[k]
        to = (me + e) % ens
        return pltpu.make_async_remote_copy(
            src_ref=l_ref.at[pl.ds(pl.multiple_of(to * circuits, circuits), circuits)],
            dst_ref=q_ref.at[k],
            send_sem=sum_send.at[k],
            recv_sem=sum_recv.at[k],
            device_id={"ens": to, "amp": (here + a) % amp},
            device_id_type=MESH_ID,
        )

    for k in range(len(everyone)):
        slab(k).start()
    result = l_ref[pl.ds(pl.multiple_of(me * circuits, circuits), circuits)]
    for k in range(len(everyone)):
        slab(k).wait_recv()
        result = result + q_ref[k]
    columns = total // amp
    result = pltpu.roll(result, (2 * half - here * columns) % (2 * half), 1)
    shape = (circuits, columns)
    row = lax.broadcasted_iota(jnp.int32, shape, 0) + me * circuits
    column = lax.broadcasted_iota(jnp.int32, shape, 1) + here * columns
    scale = jnp.where(row == column, 0.0, 1.0 / math.sqrt(rows * ORDER * amp))
    o_ref[0] = result[:, :columns] * scale
    o_ref[1] = result[:, half : half + columns] * scale

    for k in range(len(everyone)):
        slab(k).wait_send()
    for k in range(1, ens):
        gate_copy(k, me).wait_send()
        first_block(k, me).wait_send()
    for e in range(ens):
        half_copy(e, side).wait_send()

    def drain(circuit, carry):
        for k in range(len(peers)):
            piece(k, circuit, side, me).wait_send()
        return carry

    lax.fori_loop(1, circuits, drain, 0)


def fused(states, layer_angles, entangler, global_angles):
    circuits, _, local = states.shape
    rows = local // ORDER
    layers = layer_angles.shape[1]
    ens, amp = lax.axis_size("ens"), lax.axis_size("amp")
    total = ens * circuits
    share = rows // (2 * ens)
    depth = 2 * (share // 16) * 2 * ORDER
    table, angles, links = small_tables(layer_angles, entangler)
    return pl.pallas_call(
        functools.partial(fused_kernel, layers, ens, amp),
        out_shape=jax.ShapeDtypeStruct((2, circuits, total // amp), jnp.float32),
        in_specs=[pl.BlockSpec(memory_space=pl.ANY)] * 5,
        out_specs=pl.BlockSpec(memory_space=pltpu.VMEM),
        scratch_shapes=[
            pltpu.VMEM((1 + ens, 2 * ORDER, 2 * ORDER), jnp.bfloat16),
            pltpu.VMEM((1 + ens, 2 * ORDER, 2 * ORDER), jnp.bfloat16),
            pltpu.VMEM((2, 2 * ORDER, rows), jnp.bfloat16),
            pltpu.VMEM((circuits - 1, 2, local), jnp.bfloat16),
            pltpu.VMEM((circuits, rows, 2 * ORDER), jnp.bfloat16),
            pltpu.VMEM((ens, 2, ORDER * ORDER), jnp.bfloat16),
            pltpu.VMEM((ens, ORDER, 2 * ORDER), jnp.bfloat16),
            pltpu.VMEM((2, total, share, 2 * ORDER), jnp.bfloat16),
            pltpu.VMEM((ens, 8, ORDER), jnp.float32),
            pltpu.SMEM((ens, 8, ORDER), jnp.float32),
            pltpu.VMEM((total, 16, depth), jnp.bfloat16),
            pltpu.VMEM((2 * ens, 16, depth), jnp.bfloat16),
            pltpu.VMEM((total, ORDER), jnp.float32),
            pltpu.VMEM((ens * amp - 1, circuits, ORDER), jnp.float32),
            pltpu.SMEM((2 * TABLE,), jnp.float32),
            pltpu.SMEM(angles.shape, jnp.int32),
            pltpu.SMEM(links.shape, jnp.int32),
            pltpu.SMEM((2, circuits), jnp.int32),
            pltpu.VMEM(angles.shape, jnp.int32),
            pltpu.VMEM(links.shape, jnp.int32),
            pltpu.SemaphoreType.DMA((circuits,)),
            pltpu.SemaphoreType.DMA((6,)),
            pltpu.SemaphoreType.DMA((circuits, 2 * ens - 1)),
            pltpu.SemaphoreType.DMA((circuits, 2 * ens - 1)),
            pltpu.SemaphoreType.DMA((ens - 1,)),
            pltpu.SemaphoreType.DMA((ens - 1,)),
            pltpu.SemaphoreType.DMA((ens,)),
            pltpu.SemaphoreType.DMA((ens,)),
            pltpu.SemaphoreType.DMA((ens - 1,)),
            pltpu.SemaphoreType.DMA((ens - 1,)),
            pltpu.SemaphoreType.DMA((ens * amp - 1,)),
            pltpu.SemaphoreType.DMA((ens * amp - 1,)),
        ],
        compiler_params=pltpu.CompilerParams(
            vmem_limit_bytes=62 << 20, collective_id=0, has_side_effects=True
        ),
    )(table, angles, links, jnp.transpose(global_angles), states)


def finish(summed, states, circuits):
    columns = lax.axis_size("ens") * circuits // lax.axis_size("amp")
    row_index = lax.axis_index("ens") * circuits + jnp.arange(circuits, dtype=jnp.int32)
    column_index = lax.axis_index("amp") * columns + jnp.arange(columns, dtype=jnp.int32)
    off_diagonal = jnp.where(row_index[:, None] == column_index[None, :], 0.0, 1.0).astype(jnp.float32)
    amplitudes = states.shape[2] * lax.axis_size("amp")
    return summed * (off_diagonal / math.sqrt(amplitudes))[None]


def fits(states, layers):
    circuits, _, local = states.shape
    ens, amp = lax.axis_size("ens"), lax.axis_size("amp")
    rows = local // ORDER
    return (
        rows == ens * ORDER and circuits % 8 == 0 and circuits <= 16 and layers == 16 and ens * circuits <= ORDER // 2
        and ens * circuits % amp == 0 and amp >= 2 and local <= 1 << 16 and ens > 1
    )


def scaled(coefficient, amplitudes):
    real_c = coefficient[0][:, None]
    imag_c = coefficient[1][:, None]
    return jnp.stack(
        [
            real_c * amplitudes[:, 0] - imag_c * amplitudes[:, 1],
            real_c * amplitudes[:, 1] + imag_c * amplitudes[:, 0],
        ],
        1,
    )


def choose_pair(upper_side, when_lower, when_upper):
    return (
        jnp.where(upper_side == 0, when_lower[0], when_upper[0]),
        jnp.where(upper_side == 0, when_lower[1], when_upper[1]),
    )


def pair_tile(mine, remote):
    products = jnp.einsum("ipa,jqa->pqij", mine, remote, preferred_element_type=jnp.float32)
    return jnp.stack([products[0, 0] + products[1, 1], products[0, 1] - products[1, 0]])


def body(states, layer_angles, entangler, global_angles):
    circuits = states.shape[0]
    if fits(states, layer_angles.shape[1]):
        return fused(states, layer_angles, entangler, global_angles)
    turned = all_layers(states, layer_angles, entangler).reshape(circuits, -1, 2, ORDER)
    current = jnp.swapaxes(turned, 1, 2).reshape(states.shape)
    swap_bit = lax.axis_size("amp").bit_length() - 2
    upper_side = lax.axis_index("amp") // 2**swap_bit % 2
    gate = rotation(global_angles[:, 0], global_angles[:, 1])
    partner = from_partner(current, "amp", swap_bit)
    coeff_self = choose_pair(upper_side, gate[0], gate[3])
    coeff_other = choose_pair(upper_side, gate[1], gate[2])
    final_states = (
        scaled(coeff_self, current.astype(jnp.float32))
        + scaled(coeff_other, partner.astype(jnp.float32))
    ).astype(jnp.bfloat16)
    partials = pair_tile(final_states, lax.all_gather(final_states, "ens", axis=0, tiled=True))
    summed = lax.psum_scatter(partials, "amp", scatter_dimension=2, tiled=True)
    return finish(summed, states, circuits)


def solution(mesh):
    return jax.shard_map(
        body,
        mesh=mesh,
        in_specs=(
            P(("groups", "ens"), None, "amp"),
            P(("groups", "ens"), None, None, None),
            P(("groups", "ens"), None, None),
            P(("groups", "ens"), None),
        ),
        out_specs=P(None, ("groups", "ens"), "amp"),
        check_vma=False,
    )
```

```python
import functools
import math

import jax
import jax.numpy as jnp
import numpy as np
from jax import lax
from jax.experimental import pallas as pl
from jax.experimental.pallas import tpu as pltpu
from jax.sharding import PartitionSpec as P

JOINED = 7
TABLE = 64
ORDER = 2**JOINED
LOW = 3
MESH_ID = pl.DeviceIdType.MESH


def from_partner(array, axis, bit):
    return lax.ppermute(array, axis, [(i, i ^ 1 << bit) for i in range(lax.axis_size(axis))])


def rotation(polar_index, azimuth_index):
    polar = polar_index.astype(jnp.float32) * (math.pi / TABLE)
    azimuth = azimuth_index.astype(jnp.float32) * (math.pi / TABLE)
    cos_polar = jnp.cos(polar)
    sin_polar = jnp.sin(polar)
    cos_azim = jnp.cos(azimuth)
    sin_azim = jnp.sin(azimuth)
    return (
        (cos_azim * cos_polar, -sin_azim * cos_polar),
        (-cos_azim * sin_polar, sin_azim * sin_polar),
        (cos_azim * sin_polar, sin_azim * sin_polar),
        (cos_azim * cos_polar, sin_azim * cos_polar),
    )


def bit_of(shape, dim, bit, shift=0):
    return (lax.broadcasted_iota(jnp.int32, shape, dim) >> (bit - shift)) & 1


class Indexed:
    def __init__(self, circuits, circuit, table_ref, angle_ref, link_ref):
        self.circuits, self.circuit = circuits, circuit
        self.table, self.angle, self.link = table_ref, angle_ref, link_ref

    def cos_sin(self, layer, k, which):
        index = self.angle[(self.circuit * JOINED + k) * 2 + which, layer]
        return self.table[0, index], self.table[0, index + TABLE]

    def flip(self, layer, k):
        return 1.0 - 2.0 * self.link[k * self.circuits + self.circuit, layer].astype(jnp.float32)


class Listed:
    def __init__(self, ref):
        self.ref = ref

    def entry(self, r, layer):
        return self.ref[r // 8, r % 8 * 16 + layer]

    def cos_sin(self, layer, k, which):
        return self.entry(2 * k + which, layer), self.entry(2 * JOINED + 2 * k + which, layer)

    def flip(self, layer, k):
        return self.entry(4 * JOINED + k, layer)


def part_factor(tables, layer, upper, high):
    qubits = range(LOW, JOINED) if high else range(LOW)
    shape = (2 ** len(qubits), ORDER)
    shift = LOW if high else 0
    row = {k: bit_of(shape, 0, k, shift) for k in qubits}
    lane = {k: bit_of(shape, 1, k) for k in range(JOINED)}
    out = row if upper else lane
    real = imag = None
    turn = None
    for k in qubits:
        cos_t, sin_t = tables.cos_sin(layer, k, 0)
        cos_f, sin_f = tables.cos_sin(layer, k, 1)
        side = (2 * out[k] - 1).astype(jnp.float32)
        factor = jnp.where(row[k] == lane[k], cos_t, side * sin_t)
        turn = factor if turn is None else turn * factor
        step = side * sin_f
        if real is None:
            real, imag = jnp.full(shape, cos_f), step
        else:
            real, imag = real * cos_f - imag * step, real * step + imag * cos_f
    for k in range(JOINED - 1):
        inside = k in qubits and k + 1 in qubits
        if inside or (not upper and not high and k == LOW - 1):
            turn = jnp.where(out[k] * out[k + 1] == 1, tables.flip(layer, k) * turn, turn)
    return real * turn, imag * turn


def build(tables, layer, upper, w_ref):
    low_real, low_imag = part_factor(tables, layer, upper, False)
    high_real, high_imag = part_factor(tables, layer, upper, True)
    lows = [(low_real, low_imag)] * 2
    if upper:
        crossed = bit_of(low_real.shape, 0, LOW - 1) == 1
        flip = tables.flip(layer, LOW - 1)
        lows[1] = tuple(jnp.where(crossed, flip * v, v) for v in lows[0])
    for pair in range(ORDER // 16):
        reals, imags = [], []
        for odd in range(2):
            r = 2 * pair + odd
            a_real = jnp.broadcast_to(high_real[r : r + 1], (8, ORDER))
            a_imag = jnp.broadcast_to(high_imag[r : r + 1], (8, ORDER))
            b_real, b_imag = lows[odd]
            reals.append(a_real * b_real - a_imag * b_imag)
            imags.append(a_real * b_imag + a_imag * b_real)
        real = jnp.concatenate(reals, 0)
        imag = jnp.concatenate(imags, 0)
        plus, minus = imag.astype(jnp.bfloat16), (-imag).astype(jnp.bfloat16)
        real = real.astype(jnp.bfloat16)
        top, bottom = (minus, plus) if upper else (plus, minus)
        rows = pl.ds(16 * pair, 16)
        rows_below = pl.ds(ORDER + 16 * pair, 16)
        w_ref[rows, :ORDER] = real
        w_ref[rows, ORDER:] = top
        w_ref[rows_below, :ORDER] = bottom
        w_ref[rows_below, ORDER:] = real


def bridge(values):
    rows, columns = values.shape
    shape = (1, 8, columns)
    odd = bit_of(shape, 1, 0) * bit_of(shape, 2, JOINED - 1)
    sign = (1 - 2 * odd).astype(jnp.float32)
    return (values.reshape(rows // 8, 8, columns) * sign).reshape(rows, columns)


def spread(x_ref, t_ref):
    def some(step, carry):
        flat = x_ref[:, pl.ds(pl.multiple_of(step * 16 * ORDER, 16 * ORDER), 16 * ORDER)]
        tiles = flat.astype(jnp.float32).reshape(2, 16, ORDER).astype(jnp.bfloat16)
        rows_at = pl.ds(pl.multiple_of(step * 16, 16), 16)
        t_ref[rows_at, :ORDER] = tiles[0]
        t_ref[rows_at, ORDER:] = tiles[1]
        return carry

    lax.fori_loop(0, t_ref.shape[0] // 16, some, 0, unroll=4)


def run_layers(layers, chains):
    for tables, _, wl_ref, _, _ in chains:
        build(tables, 0, False, wl_ref)

    def two(pair, carry):
        layer = 2 * pair
        following = jnp.minimum(layer + 2, layers - 2)
        for tables, t_ref, wl_ref, wu_ref, s_ref in chains:
            y = jnp.dot(t_ref[...], wl_ref[...], preferred_element_type=jnp.float32)
            y = bridge(y).astype(jnp.bfloat16)
            for b in range(t_ref.shape[0] // ORDER):
                for p in range(2):
                    s_ref[p * ORDER : (p + 1) * ORDER, b * ORDER : (b + 1) * ORDER] = y[
                        b * ORDER : (b + 1) * ORDER, p * ORDER : (p + 1) * ORDER
                    ]
            build(tables, layer + 1, True, wu_ref)
        for tables, t_ref, wl_ref, wu_ref, s_ref in chains:
            y = jnp.dot(wu_ref[...], s_ref[...], preferred_element_type=jnp.float32)
            y = bridge(y).astype(jnp.bfloat16)
            for b in range(t_ref.shape[0] // ORDER):
                for p in range(2):
                    t_ref[b * ORDER : (b + 1) * ORDER, p * ORDER : (p + 1) * ORDER] = y[
                        p * ORDER : (p + 1) * ORDER, b * ORDER : (b + 1) * ORDER
                    ]
            build(tables, following, False, wl_ref)
        return carry

    lax.fori_loop(0, layers // 2, two, 0)


def layers_kernel(circuits, layers, table_ref, angle_ref, link_ref, x_ref, t_ref, wl_ref, wu_ref, s_ref):
    tables = Indexed(circuits, pl.program_id(0), table_ref, angle_ref, link_ref)
    spread(x_ref.at[0], t_ref.at[0])
    run_layers(layers, [(tables, t_ref.at[0], wl_ref, wu_ref, s_ref)])


def small_tables(layer_angles, entangler):
    circuits, layers = layer_angles.shape[:2]
    angle = np.arange(TABLE, dtype=np.float64) * (math.pi / TABLE)
    table = jnp.asarray(np.concatenate([np.cos(angle), np.sin(angle)]).astype(np.float32))[None]
    angles = jnp.transpose(layer_angles, (0, 2, 3, 1)).reshape(circuits * JOINED * 2, layers)
    links = jnp.transpose(entangler, (2, 0, 1)).reshape((JOINED - 1) * circuits, layers)
    return table, angles, links


def all_layers(states, layer_angles, entangler):
    circuits, _, local = states.shape
    rows = local // ORDER
    layers = layer_angles.shape[1]
    smem = pl.BlockSpec(memory_space=pltpu.SMEM)
    return pl.pallas_call(
        functools.partial(layers_kernel, circuits, layers),
        grid=(circuits,),
        out_shape=jax.ShapeDtypeStruct((circuits, rows, 2 * ORDER), jnp.bfloat16),
        in_specs=[smem, smem, smem, pl.BlockSpec((1, 2, local), lambda g: (g, 0, 0))],
        out_specs=pl.BlockSpec((1, rows, 2 * ORDER), lambda g: (g, 0, 0)),
        scratch_shapes=[
            pltpu.VMEM((2 * ORDER, 2 * ORDER), jnp.bfloat16),
            pltpu.VMEM((2 * ORDER, 2 * ORDER), jnp.bfloat16),
            pltpu.VMEM((2 * ORDER, rows), jnp.bfloat16),
        ],
        compiler_params=pltpu.CompilerParams(vmem_limit_bytes=32 << 20),
    )(*small_tables(layer_angles, entangler), states)


def gate_pair(gate, low, high):
    outs = []
    for r in range(2):
        a_real, a_imag, b_real, b_imag = (gate[4 * r + k] for k in range(4))
        real = a_real * low[0] - a_imag * low[1] + (b_real * high[0] - b_imag * high[1])
        imag = a_real * low[1] + a_imag * low[0] + (b_real * high[1] + b_imag * high[0])
        outs.append((real, imag))
    return outs


def exact_dot(values, picks, dims):
    total = None
    for _ in range(3):
        term = values.astype(jnp.bfloat16)
        values = values - term.astype(jnp.float32)
        operands = (term, picks) if dims[0] == "values" else (picks, term)
        part = lax.dot_general(*operands, (dims[1], ((), ())), preferred_element_type=jnp.float32)
        total = part if total is None else total + part
    return total


def listed(angles, links):
    angle = angles.astype(jnp.float32) * (math.pi / TABLE)
    layers = angle.shape[1]
    flips = 1.0 - 2.0 * links.astype(jnp.float32)
    unused = jnp.zeros((64 - 4 * JOINED - (JOINED - 1), layers), jnp.float32)
    values = jnp.concatenate([jnp.cos(angle), jnp.sin(angle), flips, unused], 0)
    shape = (layers, ORDER)
    source = lax.broadcasted_iota(jnp.int32, shape, 0)
    again = jnp.where(source == lax.broadcasted_iota(jnp.int32, shape, 1) % layers, 1.0, 0.0).astype(jnp.bfloat16)
    repeated = exact_dot(values, again, ("values", ((1,), (0,)))).reshape(8, 8, ORDER)
    shape = (1, 8, ORDER)
    mine = lax.broadcasted_iota(jnp.int32, shape, 1) == lax.broadcasted_iota(jnp.int32, shape, 2) // layers
    return jnp.where(mine, repeated, 0.0).sum(1)


GATE_ROW = 7


def fused_kernel(
    layers, ens, amp,
    angle_hbm, link_hbm, global_hbm, x_hbm, o_ref,
    wl_ref, wu_ref, s_ref, x_ref, t_ref, first_x, first_t, r_ref, c_ref, cs_ref, f_ref, h_ref, l_ref, q_ref,
    table_vmem, table_ref, angle_ref, link_ref, global_ref, angle_vmem, link_vmem,
    load_sem, small_sem, send_sem, recv_sem, first_send, first_recv, half_send, half_recv,
    gate_send, gate_recv, sum_send, sum_recv,
):
    circuits, rows, _ = t_ref.shape
    total = ens * circuits
    share = rows // (2 * ens)
    parts = share // 16
    half = 2 * ORDER // 4
    bit = amp.bit_length() - 2
    me = lax.axis_index("ens")
    here = lax.axis_index("amp")
    side = (here // 2**bit) % 2
    rest = here - side * 2**bit
    square = ORDER * ORDER

    barrier = pltpu.get_barrier_semaphore()
    everyone = [(k // amp, k % amp) for k in range(1, ens * amp)]
    everyone = sorted(everyone, key=lambda p: (abs(2 * p[0] - ens), -p[1]))
    for e, a in everyone:
        pl.semaphore_signal(
            barrier, inc=1, device_id={"ens": (me + e) % ens, "amp": (here + a) % amp}, device_id_type=MESH_ID
        )

    def load(circuit):
        return pltpu.make_async_copy(x_hbm.at[circuit], x_ref.at[circuit - 1], load_sem.at[circuit])

    def block(index):
        return x_hbm.at[0, :, pl.ds(pl.multiple_of(index * square, square), square)]

    own_block = pltpu.make_async_copy(block(me), first_x.at[me], load_sem.at[0])
    smalls = [
        pltpu.make_async_copy(source, target, small_sem.at[i])
        for i, (source, target) in enumerate(
            (
                (table_vmem, table_ref), (angle_hbm, angle_ref), (link_hbm, link_ref), (global_hbm, global_ref),
                (angle_hbm, angle_vmem), (link_hbm, link_vmem),
            )
        )
    ]
    for copy in smalls[1:]:
        copy.start()
    for circuit in range(1, circuits):
        load(circuit).start()
    own_block.start()

    def first_block(k, source):
        to = (me + k) % ens
        return pltpu.make_async_remote_copy(
            src_ref=block(to),
            dst_ref=first_x.at[source],
            send_sem=first_send.at[k - 1],
            recv_sem=first_recv.at[k - 1],
            device_id={"ens": to},
            device_id_type=MESH_ID,
        )

    far_first = sorted(range(1, ens), key=lambda k: abs(2 * k - ens))
    entry = lax.broadcasted_iota(jnp.int32, table_vmem.shape, 1)
    angle = (entry % TABLE).astype(jnp.float32) * (math.pi / TABLE)
    table_vmem[...] = jnp.where(entry < TABLE, jnp.cos(angle), jnp.sin(angle))
    smalls[0].start()
    pl.semaphore_wait(barrier, len(everyone))
    for k in far_first:
        first_block(k, me).start()

    for copy in smalls:
        copy.wait()
    links = jnp.concatenate([link_vmem[k * circuits : k * circuits + 1] for k in range(JOINED - 1)], 0)
    tile = listed(angle_vmem[: 2 * JOINED], links)
    lane = lax.broadcasted_iota(jnp.int32, (1, ORDER), 1)
    line = jnp.zeros((1, ORDER), jnp.float32)
    for circuit in range(circuits):
        polar, azimuth = global_ref[0, circuit], global_ref[1, circuit]
        cos_t, sin_t = table_ref[0, polar], table_ref[0, polar + TABLE]
        cos_f, sin_f = table_ref[0, azimuth], table_ref[0, azimuth + TABLE]
        entries = (
            cos_f * cos_t, -sin_f * cos_t, -cos_f * sin_t, sin_f * sin_t,
            cos_f * sin_t, sin_f * sin_t, cos_f * cos_t, sin_f * cos_t,
        )
        for k, entry in enumerate(entries):
            line = jnp.where(lane == circuit * 8 + k, entry, line)
    is_gate = lax.broadcasted_iota(jnp.int32, (8, ORDER), 0) == GATE_ROW
    c_ref[pl.ds(me, 1)] = jnp.where(is_gate, line, tile)[None]

    def gate_copy(k, source):
        return pltpu.make_async_remote_copy(
            src_ref=c_ref.at[source],
            dst_ref=c_ref.at[source],
            send_sem=gate_send.at[k - 1],
            recv_sem=gate_recv.at[k - 1],
            device_id={"ens": (me + k) % ens},
            device_id_type=MESH_ID,
        )

    for k in far_first:
        gate_copy(k, me).start()

    peers = sorted(((k // ens, k % ens) for k in range(1, 2 * ens)), key=lambda p: (abs(2 * p[1] - ens), p[0]))

    def piece(k, circuit, from_side, from_ens):
        across, along = peers[k]
        to_side = side + across - 2 * side * across
        to_ens = (me + along) % ens
        start = pl.multiple_of((2 * to_ens + to_side) * share, share)
        return pltpu.make_async_remote_copy(
            src_ref=t_ref.at[circuit, pl.ds(start, share)],
            dst_ref=r_ref.at[from_side, from_ens * circuits + circuit],
            send_sem=send_sem.at[circuit, k],
            recv_sem=recv_sem.at[circuit, k],
            device_id={"ens": to_ens, "amp": to_side * 2**bit + rest},
            device_id_type=MESH_ID,
        )

    def half_copy(e, from_side):
        to_side = 1 - side
        return pltpu.make_async_remote_copy(
            src_ref=first_t.at[e, pl.ds(pl.multiple_of(to_side * share, share), share)],
            dst_ref=r_ref.at[from_side, e * circuits],
            send_sem=half_send.at[e],
            recv_sem=half_recv.at[e],
            device_id={"amp": to_side * 2**bit + rest},
            device_id_type=MESH_ID,
        )

    def chain(circuit, i):
        load(circuit).wait()
        spread(x_ref.at[circuit - 1], t_ref.at[circuit])
        tables = Indexed(circuits, circuit, table_ref, angle_ref, link_ref)
        return tables, t_ref.at[circuit], wl_ref.at[i], wu_ref.at[i], s_ref.at[i]

    def send(circuit):
        for k in range(len(peers)):
            piece(k, circuit, side, me).start()
        own = pl.multiple_of((2 * me + side) * share, share)
        r_ref[side, me * circuits + circuit] = t_ref[circuit, pl.ds(own, share), :]

    def compute(pair, carry):
        both = (2 * pair + 1, 2 * pair + 2)
        run_layers(layers, [chain(circuit, i) for i, circuit in enumerate(both)])
        for circuit in both:
            send(circuit)
        return carry

    lax.fori_loop(0, circuits // 2 - 1, compute, 0)

    for k in range(1, ens):
        gate_copy(k, (me + ens - k) % ens).wait_recv()
    scalars = pltpu.make_async_copy(c_ref, cs_ref, small_sem.at[0])
    scalars.start()
    own_block.wait()
    for k in range(1, ens):
        first_block(k, (me + ens - k) % ens).wait_recv()
    for e in range(ens):
        spread(first_x.at[e], first_t.at[e])
    scalars.wait()
    last = circuits - 1
    run_layers(
        layers,
        [chain(last, 0)]
        + [
            (
                Listed(cs_ref.at[e]), first_t.at[e], wl_ref.at[1 + e], wu_ref.at[1 + e],
                s_ref.at[1, :, e * ORDER : (e + 1) * ORDER],
            )
            for e in range(ens)
        ],
    )
    send(last)
    for e in range(ens):
        half_copy(e, side).start()
        r_ref[side, e * circuits] = first_t[e, pl.ds(pl.multiple_of(side * share, share), share), :]

    f_ref[...] = jnp.zeros_like(f_ref)
    l_ref[...] = jnp.zeros_like(l_ref)

    depth = f_ref.shape[2]

    def gram(circuit, carry):
        @pl.when(circuit == 0)
        def _():
            for e in range(ens):
                half_copy(e, 1 - side).wait_recv()

        @pl.when(circuit != 0)
        def _():
            for k, (across, along) in enumerate(peers):
                piece(k, circuit, side + across - 2 * side * across, (me + ens - along) % ens).wait_recv()

        for e in range(ens):
            which = e * circuits + circuit
            gate = [cs_ref[e, GATE_ROW, circuit * 8 + k] for k in range(8)]
            low = r_ref[0, which].astype(jnp.float32)
            high = r_ref[1, which].astype(jnp.float32)
            outs = gate_pair(gate, (low[:, :ORDER], low[:, ORDER:]), (high[:, :ORDER], high[:, ORDER:]))
            for x, (real, imag) in enumerate(outs):
                real = real.astype(jnp.bfloat16)
                imag = imag.astype(jnp.bfloat16)
                minus = -real
                for part in range(parts):
                    at = (x * parts + part) * 2 * ORDER
                    take = slice(16 * part, 16 * part + 16)
                    for ref, row in ((f_ref, which), (h_ref, e)):
                        ref[row, :, at : at + ORDER] = real[take]
                        ref[row, :, at + ORDER : at + 2 * ORDER] = imag[take]
                    h_ref[ens + e, :, at : at + ORDER] = imag[take]
                    h_ref[ens + e, :, at + ORDER : at + 2 * ORDER] = minus[take]
        fresh = 2 * ens * 16
        full = lax.dot_general(
            f_ref[...].reshape(total * 16, depth), h_ref[...].reshape(fresh, depth),
            (((1,), (1,)), ((), ())), preferred_element_type=jnp.float32,
        )
        shape = (1, 16, fresh)
        same = lax.broadcasted_iota(jnp.int32, shape, 1) == lax.broadcasted_iota(jnp.int32, shape, 2) % 16
        kept = jnp.where(same, full.reshape(total, 16, fresh), 0.0).sum(1)

        shape = (fresh, ORDER)
        source = lax.broadcasted_iota(jnp.int32, shape, 0) // 16
        target = lax.broadcasted_iota(jnp.int32, shape, 1)
        place = jnp.where(source >= ens, half + (source - ens) * circuits, source * circuits) + circuit
        above = exact_dot(kept, jnp.where(place == target, 1.0, 0.0).astype(jnp.bfloat16), ("values", ((1,), (0,))))

        shape = (half, fresh)
        row = lax.broadcasted_iota(jnp.int32, shape, 0)
        is_imag = lax.broadcasted_iota(jnp.int32, shape, 1) // 16 >= ens
        before = (row % circuits < circuit) & (row < total)
        doubled = kept if total == half else jnp.concatenate([kept, jnp.zeros((half - total, fresh), jnp.float32)], 0)
        stacked = jnp.concatenate(
            [jnp.where(before & ~is_imag, doubled, 0.0), jnp.where(before & is_imag, -doubled, 0.0)], 0
        )
        shape = (total, fresh)
        row = lax.broadcasted_iota(jnp.int32, shape, 0)
        source = lax.broadcasted_iota(jnp.int32, shape, 1) // 16 % ens
        gather = jnp.where(row == source * circuits + circuit, 1.0, 0.0).astype(jnp.bfloat16)
        mirrored = exact_dot(stacked, gather, ("picks", ((1,), (1,))))
        l_ref[...] += above + mirrored
        return carry

    lax.fori_loop(0, circuits, gram, 0)

    def slab(k):
        e, a = everyone[k]
        to = (me + e) % ens
        return pltpu.make_async_remote_copy(
            src_ref=l_ref.at[pl.ds(pl.multiple_of(to * circuits, circuits), circuits)],
            dst_ref=q_ref.at[k],
            send_sem=sum_send.at[k],
            recv_sem=sum_recv.at[k],
            device_id={"ens": to, "amp": (here + a) % amp},
            device_id_type=MESH_ID,
        )

    for k in range(len(everyone)):
        slab(k).start()
    result = l_ref[pl.ds(pl.multiple_of(me * circuits, circuits), circuits)]
    for k in range(len(everyone)):
        slab(k).wait_recv()
        result = result + q_ref[k]
    columns = total // amp
    result = pltpu.roll(result, (2 * half - here * columns) % (2 * half), 1)
    shape = (circuits, columns)
    row = lax.broadcasted_iota(jnp.int32, shape, 0) + me * circuits
    column = lax.broadcasted_iota(jnp.int32, shape, 1) + here * columns
    scale = jnp.where(row == column, 0.0, 1.0 / math.sqrt(rows * ORDER * amp))
    o_ref[0] = result[:, :columns] * scale
    o_ref[1] = result[:, half : half + columns] * scale

    for k in range(len(everyone)):
        slab(k).wait_send()
    for k in range(1, ens):
        gate_copy(k, me).wait_send()
        first_block(k, me).wait_send()
    for e in range(ens):
        half_copy(e, side).wait_send()

    def drain(circuit, carry):
        for k in range(len(peers)):
            piece(k, circuit, side, me).wait_send()
        return carry

    lax.fori_loop(1, circuits, drain, 0)


def fused(states, layer_angles, entangler, global_angles):
    circuits, _, local = states.shape
    rows = local // ORDER
    layers = layer_angles.shape[1]
    ens, amp = lax.axis_size("ens"), lax.axis_size("amp")
    total = ens * circuits
    share = rows // (2 * ens)
    depth = 2 * (share // 16) * 2 * ORDER
    _, angles, links = small_tables(layer_angles, entangler)
    return pl.pallas_call(
        functools.partial(fused_kernel, layers, ens, amp),
        out_shape=jax.ShapeDtypeStruct((2, circuits, total // amp), jnp.float32),
        in_specs=[pl.BlockSpec(memory_space=pl.ANY)] * 4,
        out_specs=pl.BlockSpec(memory_space=pltpu.VMEM),
        scratch_shapes=[
            pltpu.VMEM((1 + ens, 2 * ORDER, 2 * ORDER), jnp.bfloat16),
            pltpu.VMEM((1 + ens, 2 * ORDER, 2 * ORDER), jnp.bfloat16),
            pltpu.VMEM((2, 2 * ORDER, rows), jnp.bfloat16),
            pltpu.VMEM((circuits - 1, 2, local), jnp.bfloat16),
            pltpu.VMEM((circuits, rows, 2 * ORDER), jnp.bfloat16),
            pltpu.VMEM((ens, 2, ORDER * ORDER), jnp.bfloat16),
            pltpu.VMEM((ens, ORDER, 2 * ORDER), jnp.bfloat16),
            pltpu.VMEM((2, total, share, 2 * ORDER), jnp.bfloat16),
            pltpu.VMEM((ens, 8, ORDER), jnp.float32),
            pltpu.SMEM((ens, 8, ORDER), jnp.float32),
            pltpu.VMEM((total, 16, depth), jnp.bfloat16),
            pltpu.VMEM((2 * ens, 16, depth), jnp.bfloat16),
            pltpu.VMEM((total, ORDER), jnp.float32),
            pltpu.VMEM((ens * amp - 1, circuits, ORDER), jnp.float32),
            pltpu.VMEM((1, 2 * TABLE), jnp.float32),
            pltpu.SMEM((1, 2 * TABLE), jnp.float32),
            pltpu.SMEM(angles.shape, jnp.int32),
            pltpu.SMEM(links.shape, jnp.int32),
            pltpu.SMEM((2, circuits), jnp.int32),
            pltpu.VMEM(angles.shape, jnp.int32),
            pltpu.VMEM(links.shape, jnp.int32),
            pltpu.SemaphoreType.DMA((circuits,)),
            pltpu.SemaphoreType.DMA((6,)),
            pltpu.SemaphoreType.DMA((circuits, 2 * ens - 1)),
            pltpu.SemaphoreType.DMA((circuits, 2 * ens - 1)),
            pltpu.SemaphoreType.DMA((ens - 1,)),
            pltpu.SemaphoreType.DMA((ens - 1,)),
            pltpu.SemaphoreType.DMA((ens,)),
            pltpu.SemaphoreType.DMA((ens,)),
            pltpu.SemaphoreType.DMA((ens - 1,)),
            pltpu.SemaphoreType.DMA((ens - 1,)),
            pltpu.SemaphoreType.DMA((ens * amp - 1,)),
            pltpu.SemaphoreType.DMA((ens * amp - 1,)),
        ],
        compiler_params=pltpu.CompilerParams(
            vmem_limit_bytes=55208 << 10, collective_id=0, has_side_effects=True
        ),
    )(angles, links, jnp.transpose(global_angles), states)


def finish(summed, states, circuits):
    columns = lax.axis_size("ens") * circuits // lax.axis_size("amp")
    row_index = lax.axis_index("ens") * circuits + jnp.arange(circuits, dtype=jnp.int32)
    column_index = lax.axis_index("amp") * columns + jnp.arange(columns, dtype=jnp.int32)
    off_diagonal = jnp.where(row_index[:, None] == column_index[None, :], 0.0, 1.0).astype(jnp.float32)
    amplitudes = states.shape[2] * lax.axis_size("amp")
    return summed * (off_diagonal / math.sqrt(amplitudes))[None]


def fits(states, layers):
    circuits, _, local = states.shape
    ens, amp = lax.axis_size("ens"), lax.axis_size("amp")
    rows = local // ORDER
    return (
        rows == ens * ORDER and circuits % 8 == 0 and circuits <= 16 and layers == 16 and ens * circuits <= ORDER // 2
        and ens * circuits % amp == 0 and amp >= 2 and local <= 1 << 16 and ens > 1
    )


def scaled(coefficient, amplitudes):
    real_c = coefficient[0][:, None]
    imag_c = coefficient[1][:, None]
    return jnp.stack(
        [
            real_c * amplitudes[:, 0] - imag_c * amplitudes[:, 1],
            real_c * amplitudes[:, 1] + imag_c * amplitudes[:, 0],
        ],
        1,
    )


def choose_pair(upper_side, when_lower, when_upper):
    return (
        jnp.where(upper_side == 0, when_lower[0], when_upper[0]),
        jnp.where(upper_side == 0, when_lower[1], when_upper[1]),
    )


def pair_tile(mine, remote):
    products = jnp.einsum("ipa,jqa->pqij", mine, remote, preferred_element_type=jnp.float32)
    return jnp.stack([products[0, 0] + products[1, 1], products[0, 1] - products[1, 0]])


def body(states, layer_angles, entangler, global_angles):
    circuits = states.shape[0]
    if fits(states, layer_angles.shape[1]):
        return fused(states, layer_angles, entangler, global_angles)
    turned = all_layers(states, layer_angles, entangler).reshape(circuits, -1, 2, ORDER)
    current = jnp.swapaxes(turned, 1, 2).reshape(states.shape)
    swap_bit = lax.axis_size("amp").bit_length() - 2
    upper_side = lax.axis_index("amp") // 2**swap_bit % 2
    gate = rotation(global_angles[:, 0], global_angles[:, 1])
    partner = from_partner(current, "amp", swap_bit)
    coeff_self = choose_pair(upper_side, gate[0], gate[3])
    coeff_other = choose_pair(upper_side, gate[1], gate[2])
    final_states = (
        scaled(coeff_self, current.astype(jnp.float32))
        + scaled(coeff_other, partner.astype(jnp.float32))
    ).astype(jnp.bfloat16)
    partials = pair_tile(final_states, lax.all_gather(final_states, "ens", axis=0, tiled=True))
    summed = lax.psum_scatter(partials, "amp", scatter_dimension=2, tiled=True)
    return finish(summed, states, circuits)


def solution(mesh):
    return jax.shard_map(
        body,
        mesh=mesh,
        in_specs=(
            P(("groups", "ens"), None, "amp"),
            P(("groups", "ens"), None, None, None),
            P(("groups", "ens"), None, None),
            P(("groups", "ens"), None),
        ),
        out_specs=P(None, ("groups", "ens"), "amp"),
        check_vma=False,
    )
```

```python
import functools
import math

import jax
import jax.numpy as jnp
import numpy as np
from jax import lax
from jax.experimental import pallas as pl
from jax.experimental.pallas import tpu as pltpu
from jax.sharding import PartitionSpec as P

JOINED = 7
TABLE = 64
ORDER = 2**JOINED
LOW = 3
MESH_ID = pl.DeviceIdType.MESH


def from_partner(array, axis, bit):
    return lax.ppermute(array, axis, [(i, i ^ 1 << bit) for i in range(lax.axis_size(axis))])


def rotation(polar_index, azimuth_index):
    polar = polar_index.astype(jnp.float32) * (math.pi / TABLE)
    azimuth = azimuth_index.astype(jnp.float32) * (math.pi / TABLE)
    cos_polar = jnp.cos(polar)
    sin_polar = jnp.sin(polar)
    cos_azim = jnp.cos(azimuth)
    sin_azim = jnp.sin(azimuth)
    return (
        (cos_azim * cos_polar, -sin_azim * cos_polar),
        (-cos_azim * sin_polar, sin_azim * sin_polar),
        (cos_azim * sin_polar, sin_azim * sin_polar),
        (cos_azim * cos_polar, sin_azim * cos_polar),
    )


def bit_of(shape, dim, bit, shift=0):
    return (lax.broadcasted_iota(jnp.int32, shape, dim) >> (bit - shift)) & 1


class Indexed:
    def __init__(self, circuits, circuit, table_ref, angle_ref, link_ref):
        self.circuits, self.circuit = circuits, circuit
        self.table, self.angle, self.link = table_ref, angle_ref, link_ref

    def cos_sin(self, layer, k, which):
        index = self.angle[(self.circuit * JOINED + k) * 2 + which, layer]
        return self.table[0, index], self.table[0, index + TABLE]

    def flip(self, layer, k):
        return 1.0 - 2.0 * self.link[k * self.circuits + self.circuit, layer].astype(jnp.float32)


class Listed:
    def __init__(self, ref):
        self.ref = ref

    def entry(self, r, layer):
        return self.ref[r // 8, r % 8 * 16 + layer]

    def cos_sin(self, layer, k, which):
        return self.entry(2 * k + which, layer), self.entry(2 * JOINED + 2 * k + which, layer)

    def flip(self, layer, k):
        return self.entry(4 * JOINED + k, layer)


def part_factor(tables, layer, upper, high):
    qubits = range(LOW, JOINED) if high else range(LOW)
    shape = (2 ** len(qubits), ORDER)
    shift = LOW if high else 0
    row = {k: bit_of(shape, 0, k, shift) for k in qubits}
    lane = {k: bit_of(shape, 1, k) for k in range(JOINED)}
    out = row if upper else lane
    real = imag = None
    turn = None
    for k in qubits:
        cos_t, sin_t = tables.cos_sin(layer, k, 0)
        cos_f, sin_f = tables.cos_sin(layer, k, 1)
        side = (2 * out[k] - 1).astype(jnp.float32)
        factor = jnp.where(row[k] == lane[k], cos_t, side * sin_t)
        turn = factor if turn is None else turn * factor
        step = side * sin_f
        if real is None:
            real, imag = jnp.full(shape, cos_f), step
        else:
            real, imag = real * cos_f - imag * step, real * step + imag * cos_f
    for k in range(JOINED - 1):
        inside = k in qubits and k + 1 in qubits
        if inside or (not upper and not high and k == LOW - 1):
            turn = jnp.where(out[k] * out[k + 1] == 1, tables.flip(layer, k) * turn, turn)
    return real * turn, imag * turn


def build(tables, layer, upper, w_ref):
    low_real, low_imag = part_factor(tables, layer, upper, False)
    high_real, high_imag = part_factor(tables, layer, upper, True)
    lows = [(low_real, low_imag)] * 2
    if upper:
        crossed = bit_of(low_real.shape, 0, LOW - 1) == 1
        flip = tables.flip(layer, LOW - 1)
        lows[1] = tuple(jnp.where(crossed, flip * v, v) for v in lows[0])
    for pair in range(ORDER // 16):
        reals, imags = [], []
        for odd in range(2):
            r = 2 * pair + odd
            a_real = jnp.broadcast_to(high_real[r : r + 1], (8, ORDER))
            a_imag = jnp.broadcast_to(high_imag[r : r + 1], (8, ORDER))
            b_real, b_imag = lows[odd]
            reals.append(a_real * b_real - a_imag * b_imag)
            imags.append(a_real * b_imag + a_imag * b_real)
        real = jnp.concatenate(reals, 0)
        imag = jnp.concatenate(imags, 0)
        plus, minus = imag.astype(jnp.bfloat16), (-imag).astype(jnp.bfloat16)
        real = real.astype(jnp.bfloat16)
        top, bottom = (minus, plus) if upper else (plus, minus)
        rows = pl.ds(16 * pair, 16)
        rows_below = pl.ds(ORDER + 16 * pair, 16)
        w_ref[rows, :ORDER] = real
        w_ref[rows, ORDER:] = top
        w_ref[rows_below, :ORDER] = bottom
        w_ref[rows_below, ORDER:] = real


def bridge(values):
    rows, columns = values.shape
    shape = (1, 8, columns)
    odd = bit_of(shape, 1, 0) * bit_of(shape, 2, JOINED - 1)
    sign = (1 - 2 * odd).astype(jnp.float32)
    return (values.reshape(rows // 8, 8, columns) * sign).reshape(rows, columns)


def spread(x_ref, t_ref):
    def some(step, carry):
        flat = x_ref[:, pl.ds(pl.multiple_of(step * 16 * ORDER, 16 * ORDER), 16 * ORDER)]
        tiles = flat.astype(jnp.float32).reshape(2, 16, ORDER).astype(jnp.bfloat16)
        rows_at = pl.ds(pl.multiple_of(step * 16, 16), 16)
        t_ref[rows_at, :ORDER] = tiles[0]
        t_ref[rows_at, ORDER:] = tiles[1]
        return carry

    lax.fori_loop(0, t_ref.shape[0] // 16, some, 0, unroll=4)


def run_layers(layers, chains):
    for tables, _, wl_ref, _, _ in chains:
        build(tables, 0, False, wl_ref)

    def two(pair, carry):
        layer = 2 * pair
        following = jnp.minimum(layer + 2, layers - 2)
        for tables, t_ref, wl_ref, wu_ref, s_ref in chains:
            y = jnp.dot(t_ref[...], wl_ref[...], preferred_element_type=jnp.float32)
            y = bridge(y).astype(jnp.bfloat16)
            for b in range(t_ref.shape[0] // ORDER):
                for p in range(2):
                    s_ref[p * ORDER : (p + 1) * ORDER, b * ORDER : (b + 1) * ORDER] = y[
                        b * ORDER : (b + 1) * ORDER, p * ORDER : (p + 1) * ORDER
                    ]
            build(tables, layer + 1, True, wu_ref)
        for tables, t_ref, wl_ref, wu_ref, s_ref in chains:
            y = jnp.dot(wu_ref[...], s_ref[...], preferred_element_type=jnp.float32)
            y = bridge(y).astype(jnp.bfloat16)
            for b in range(t_ref.shape[0] // ORDER):
                for p in range(2):
                    t_ref[b * ORDER : (b + 1) * ORDER, p * ORDER : (p + 1) * ORDER] = y[
                        p * ORDER : (p + 1) * ORDER, b * ORDER : (b + 1) * ORDER
                    ]
            build(tables, following, False, wl_ref)
        return carry

    lax.fori_loop(0, layers // 2, two, 0)


def layers_kernel(circuits, layers, table_ref, angle_ref, link_ref, x_ref, t_ref, wl_ref, wu_ref, s_ref):
    tables = Indexed(circuits, pl.program_id(0), table_ref, angle_ref, link_ref)
    spread(x_ref.at[0], t_ref.at[0])
    run_layers(layers, [(tables, t_ref.at[0], wl_ref, wu_ref, s_ref)])


def small_tables(layer_angles, entangler):
    circuits, layers = layer_angles.shape[:2]
    angle = np.arange(TABLE, dtype=np.float64) * (math.pi / TABLE)
    table = jnp.asarray(np.concatenate([np.cos(angle), np.sin(angle)]).astype(np.float32))[None]
    angles = jnp.transpose(layer_angles, (0, 2, 3, 1)).reshape(circuits * JOINED * 2, layers)
    links = jnp.transpose(entangler, (2, 0, 1)).reshape((JOINED - 1) * circuits, layers)
    return table, angles, links


def all_layers(states, layer_angles, entangler):
    circuits, _, local = states.shape
    rows = local // ORDER
    layers = layer_angles.shape[1]
    smem = pl.BlockSpec(memory_space=pltpu.SMEM)
    return pl.pallas_call(
        functools.partial(layers_kernel, circuits, layers),
        grid=(circuits,),
        out_shape=jax.ShapeDtypeStruct((circuits, rows, 2 * ORDER), jnp.bfloat16),
        in_specs=[smem, smem, smem, pl.BlockSpec((1, 2, local), lambda g: (g, 0, 0))],
        out_specs=pl.BlockSpec((1, rows, 2 * ORDER), lambda g: (g, 0, 0)),
        scratch_shapes=[
            pltpu.VMEM((2 * ORDER, 2 * ORDER), jnp.bfloat16),
            pltpu.VMEM((2 * ORDER, 2 * ORDER), jnp.bfloat16),
            pltpu.VMEM((2 * ORDER, rows), jnp.bfloat16),
        ],
        compiler_params=pltpu.CompilerParams(vmem_limit_bytes=32 << 20),
    )(*small_tables(layer_angles, entangler), states)


def gate_pair(gate, low, high):
    outs = []
    for r in range(2):
        a_real, a_imag, b_real, b_imag = (gate[4 * r + k] for k in range(4))
        real = a_real * low[0] - a_imag * low[1] + (b_real * high[0] - b_imag * high[1])
        imag = a_real * low[1] + a_imag * low[0] + (b_real * high[1] + b_imag * high[0])
        outs.append((real, imag))
    return outs


def exact_dot(values, picks, dims):
    total = None
    for _ in range(3):
        term = values.astype(jnp.bfloat16)
        values = values - term.astype(jnp.float32)
        operands = (term, picks) if dims[0] == "values" else (picks, term)
        part = lax.dot_general(*operands, (dims[1], ((), ())), preferred_element_type=jnp.float32)
        total = part if total is None else total + part
    return total


def listed(angles, links):
    angle = angles.astype(jnp.float32) * (math.pi / TABLE)
    layers = angle.shape[1]
    flips = 1.0 - 2.0 * links.astype(jnp.float32)
    unused = jnp.zeros((64 - 4 * JOINED - (JOINED - 1), layers), jnp.float32)
    values = jnp.concatenate([jnp.cos(angle), jnp.sin(angle), flips, unused], 0)
    shape = (layers, ORDER)
    source = lax.broadcasted_iota(jnp.int32, shape, 0)
    again = jnp.where(source == lax.broadcasted_iota(jnp.int32, shape, 1) % layers, 1.0, 0.0).astype(jnp.bfloat16)
    repeated = exact_dot(values, again, ("values", ((1,), (0,)))).reshape(8, 8, ORDER)
    shape = (1, 8, ORDER)
    mine = lax.broadcasted_iota(jnp.int32, shape, 1) == lax.broadcasted_iota(jnp.int32, shape, 2) // layers
    return jnp.where(mine, repeated, 0.0).sum(1)


GATE_ROW = 7


def two_terms(values):
    first = values.astype(jnp.bfloat16)
    return jnp.concatenate([first, (values - first.astype(jnp.float32)).astype(jnp.bfloat16)], 0)


def fused_kernel(
    layers, ens, amp,
    angle_hbm, link_hbm, global_hbm, x_hbm, o_ref,
    wl_ref, wu_ref, s_ref, x_ref, t_ref, first_x, first_t, r_ref, c_ref, cs_ref, f_ref, h_ref, l_ref, q_ref,
    table_vmem, table_ref, angle_ref, link_ref, global_ref, angle_vmem, link_vmem,
    load_sem, small_sem, send_sem, recv_sem, first_send, first_recv, half_send, half_recv,
    gate_send, gate_recv, sum_send, sum_recv,
):
    circuits, rows, _ = t_ref.shape
    total = ens * circuits
    share = rows // (2 * ens)
    parts = share // 16
    half = 2 * ORDER // 4
    bit = amp.bit_length() - 2
    me = lax.axis_index("ens")
    here = lax.axis_index("amp")
    side = (here // 2**bit) % 2
    rest = here - side * 2**bit
    square = ORDER * ORDER

    barrier = pltpu.get_barrier_semaphore()
    everyone = [(k // amp, k % amp) for k in range(1, ens * amp)]
    everyone = sorted(everyone, key=lambda p: (abs(2 * p[0] - ens), -p[1]))
    for e, a in everyone:
        pl.semaphore_signal(
            barrier, inc=1, device_id={"ens": (me + e) % ens, "amp": (here + a) % amp}, device_id_type=MESH_ID
        )

    def load(circuit):
        return pltpu.make_async_copy(x_hbm.at[circuit], x_ref.at[circuit - 1], load_sem.at[circuit])

    def block(index):
        return x_hbm.at[0, :, pl.ds(pl.multiple_of(index * square, square), square)]

    own_block = pltpu.make_async_copy(block(me), first_x.at[me], load_sem.at[0])
    smalls = [
        pltpu.make_async_copy(source, target, small_sem.at[i])
        for i, (source, target) in enumerate(
            (
                (table_vmem, table_ref), (angle_hbm, angle_ref), (link_hbm, link_ref), (global_hbm, global_ref),
                (angle_hbm, angle_vmem), (link_hbm, link_vmem),
            )
        )
    ]
    for copy in smalls[1:]:
        copy.start()
    for circuit in range(1, circuits):
        load(circuit).start()
    own_block.start()

    def first_block(k, source):
        to = (me + k) % ens
        return pltpu.make_async_remote_copy(
            src_ref=block(to),
            dst_ref=first_x.at[source],
            send_sem=first_send.at[k - 1],
            recv_sem=first_recv.at[k - 1],
            device_id={"ens": to},
            device_id_type=MESH_ID,
        )

    far_first = sorted(range(1, ens), key=lambda k: abs(2 * k - ens))
    entry = lax.broadcasted_iota(jnp.int32, table_vmem.shape, 1)
    angle = (entry % TABLE).astype(jnp.float32) * (math.pi / TABLE)
    table_vmem[...] = jnp.where(entry < TABLE, jnp.cos(angle), jnp.sin(angle))
    smalls[0].start()
    pl.semaphore_wait(barrier, len(everyone))
    for k in far_first:
        first_block(k, me).start()

    for copy in smalls:
        copy.wait()
    links = jnp.concatenate([link_vmem[k * circuits : k * circuits + 1] for k in range(JOINED - 1)], 0)
    tile = listed(angle_vmem[: 2 * JOINED], links)
    lane = lax.broadcasted_iota(jnp.int32, (1, ORDER), 1)
    line = jnp.zeros((1, ORDER), jnp.float32)
    for circuit in range(circuits):
        polar, azimuth = global_ref[0, circuit], global_ref[1, circuit]
        cos_t, sin_t = table_ref[0, polar], table_ref[0, polar + TABLE]
        cos_f, sin_f = table_ref[0, azimuth], table_ref[0, azimuth + TABLE]
        entries = (
            cos_f * cos_t, -sin_f * cos_t, -cos_f * sin_t, sin_f * sin_t,
            cos_f * sin_t, sin_f * sin_t, cos_f * cos_t, sin_f * cos_t,
        )
        for k, entry in enumerate(entries):
            line = jnp.where(lane == circuit * 8 + k, entry, line)
    is_gate = lax.broadcasted_iota(jnp.int32, (8, ORDER), 0) == GATE_ROW
    c_ref[pl.ds(me, 1)] = jnp.where(is_gate, line, tile)[None]

    def gate_copy(k, source):
        return pltpu.make_async_remote_copy(
            src_ref=c_ref.at[source],
            dst_ref=c_ref.at[source],
            send_sem=gate_send.at[k - 1],
            recv_sem=gate_recv.at[k - 1],
            device_id={"ens": (me + k) % ens},
            device_id_type=MESH_ID,
        )

    for k in far_first:
        gate_copy(k, me).start()

    peers = sorted(((k // ens, k % ens) for k in range(1, 2 * ens)), key=lambda p: (abs(2 * p[1] - ens), p[0]))

    def piece(k, circuit, from_side, from_ens):
        across, along = peers[k]
        to_side = side + across - 2 * side * across
        to_ens = (me + along) % ens
        start = pl.multiple_of((2 * to_ens + to_side) * share, share)
        return pltpu.make_async_remote_copy(
            src_ref=t_ref.at[circuit, pl.ds(start, share)],
            dst_ref=r_ref.at[from_side, from_ens * circuits + circuit],
            send_sem=send_sem.at[circuit, k],
            recv_sem=recv_sem.at[circuit, k],
            device_id={"ens": to_ens, "amp": to_side * 2**bit + rest},
            device_id_type=MESH_ID,
        )

    def half_copy(e, from_side):
        to_side = 1 - side
        return pltpu.make_async_remote_copy(
            src_ref=first_t.at[e, pl.ds(pl.multiple_of(to_side * share, share), share)],
            dst_ref=r_ref.at[from_side, e * circuits],
            send_sem=half_send.at[e],
            recv_sem=half_recv.at[e],
            device_id={"amp": to_side * 2**bit + rest},
            device_id_type=MESH_ID,
        )

    def chain(circuit, i):
        load(circuit).wait()
        spread(x_ref.at[circuit - 1], t_ref.at[circuit])
        tables = Indexed(circuits, circuit, table_ref, angle_ref, link_ref)
        return tables, t_ref.at[circuit], wl_ref.at[i], wu_ref.at[i], s_ref.at[i]

    def send(circuit):
        for k in range(len(peers)):
            piece(k, circuit, side, me).start()
        own = pl.multiple_of((2 * me + side) * share, share)
        r_ref[side, me * circuits + circuit] = t_ref[circuit, pl.ds(own, share), :]

    def compute(pair, carry):
        both = (2 * pair + 1, 2 * pair + 2)
        run_layers(layers, [chain(circuit, i) for i, circuit in enumerate(both)])
        for circuit in both:
            send(circuit)
        return carry

    lax.fori_loop(0, circuits // 2 - 1, compute, 0)

    for k in range(1, ens):
        gate_copy(k, (me + ens - k) % ens).wait_recv()
    scalars = pltpu.make_async_copy(c_ref, cs_ref, small_sem.at[0])
    scalars.start()
    own_block.wait()
    for k in range(1, ens):
        first_block(k, (me + ens - k) % ens).wait_recv()
    for e in range(ens):
        spread(first_x.at[e], first_t.at[e])
    scalars.wait()
    last = circuits - 1
    run_layers(
        layers,
        [chain(last, 0)]
        + [
            (
                Listed(cs_ref.at[e]), first_t.at[e], wl_ref.at[1 + e], wu_ref.at[1 + e],
                s_ref.at[1, :, e * ORDER : (e + 1) * ORDER],
            )
            for e in range(ens)
        ],
    )
    send(last)
    for e in range(ens):
        half_copy(e, side).start()
        r_ref[side, e * circuits] = first_t[e, pl.ds(pl.multiple_of(side * share, share), share), :]

    f_ref[...] = jnp.zeros_like(f_ref)
    l_ref[...] = jnp.zeros_like(l_ref)

    depth = f_ref.shape[2]

    def gram(circuit, carry):
        @pl.when(circuit == 0)
        def _():
            for e in range(ens):
                half_copy(e, 1 - side).wait_recv()

        @pl.when(circuit != 0)
        def _():
            for k, (across, along) in enumerate(peers):
                piece(k, circuit, side + across - 2 * side * across, (me + ens - along) % ens).wait_recv()

        for e in range(ens):
            which = e * circuits + circuit
            gate = [cs_ref[e, GATE_ROW, circuit * 8 + k] for k in range(8)]
            low = r_ref[0, which].astype(jnp.float32)
            high = r_ref[1, which].astype(jnp.float32)
            outs = gate_pair(gate, (low[:, :ORDER], low[:, ORDER:]), (high[:, :ORDER], high[:, ORDER:]))
            for x, (real, imag) in enumerate(outs):
                real = real.astype(jnp.bfloat16)
                imag = imag.astype(jnp.bfloat16)
                minus = -real
                for part in range(parts):
                    at = (x * parts + part) * 2 * ORDER
                    take = slice(16 * part, 16 * part + 16)
                    for ref, row in ((f_ref, which), (h_ref, e)):
                        ref[row, :, at : at + ORDER] = real[take]
                        ref[row, :, at + ORDER : at + 2 * ORDER] = imag[take]
                    h_ref[ens + e, :, at : at + ORDER] = imag[take]
                    h_ref[ens + e, :, at + ORDER : at + 2 * ORDER] = minus[take]
        fresh = 2 * ens * 16
        full = lax.dot_general(
            f_ref[...].reshape(total * 16, depth), h_ref[...].reshape(fresh, depth),
            (((1,), (1,)), ((), ())), preferred_element_type=jnp.float32,
        )
        shape = (1, 16, fresh)
        same = lax.broadcasted_iota(jnp.int32, shape, 1) == lax.broadcasted_iota(jnp.int32, shape, 2) % 16
        kept = jnp.where(same, full.reshape(total, 16, fresh), 0.0).sum(1)

        shape = (fresh, ORDER)
        source = lax.broadcasted_iota(jnp.int32, shape, 0) // 16
        target = lax.broadcasted_iota(jnp.int32, shape, 1)
        place = jnp.where(source >= ens, half + (source - ens) * circuits, source * circuits) + circuit
        picks = jnp.where(place == target, 1.0, 0.0).astype(jnp.bfloat16)
        above = jnp.dot(two_terms(kept), picks, preferred_element_type=jnp.float32)

        shape = (half, fresh)
        row = lax.broadcasted_iota(jnp.int32, shape, 0)
        is_imag = lax.broadcasted_iota(jnp.int32, shape, 1) // 16 >= ens
        before = (row % circuits < circuit) & (row < total)
        doubled = kept if total == half else jnp.concatenate([kept, jnp.zeros((half - total, fresh), jnp.float32)], 0)
        stacked = jnp.concatenate(
            [jnp.where(before & ~is_imag, doubled, 0.0), jnp.where(before & is_imag, -doubled, 0.0)], 0
        )
        shape = (total, fresh)
        row = lax.broadcasted_iota(jnp.int32, shape, 0)
        source = lax.broadcasted_iota(jnp.int32, shape, 1) // 16 % ens
        gather = jnp.where(row == source * circuits + circuit, 1.0, 0.0).astype(jnp.bfloat16)
        mirrored = lax.dot_general(
            gather, two_terms(stacked), (((1,), (1,)), ((), ())), preferred_element_type=jnp.float32
        )
        l_ref[...] += above[:total] + above[total:] + (mirrored[:, :ORDER] + mirrored[:, ORDER:])
        return carry

    lax.fori_loop(0, circuits, gram, 0)

    def slab(k):
        e, a = everyone[k]
        to = (me + e) % ens
        return pltpu.make_async_remote_copy(
            src_ref=l_ref.at[pl.ds(pl.multiple_of(to * circuits, circuits), circuits)],
            dst_ref=q_ref.at[k],
            send_sem=sum_send.at[k],
            recv_sem=sum_recv.at[k],
            device_id={"ens": to, "amp": (here + a) % amp},
            device_id_type=MESH_ID,
        )

    for k in range(len(everyone)):
        slab(k).start()
    for k in range(1, ens):
        gate_copy(k, me).wait_send()
        first_block(k, me).wait_send()
    for e in range(ens):
        half_copy(e, side).wait_send()

    def drain(circuit, carry):
        for k in range(len(peers)):
            piece(k, circuit, side, me).wait_send()
        return carry

    lax.fori_loop(1, circuits, drain, 0)

    result = l_ref[pl.ds(pl.multiple_of(me * circuits, circuits), circuits)]
    for k in range(len(everyone)):
        slab(k).wait_recv()
        result = result + q_ref[k]
    columns = total // amp
    result = pltpu.roll(result, (2 * half - here * columns) % (2 * half), 1)
    shape = (circuits, columns)
    row = lax.broadcasted_iota(jnp.int32, shape, 0) + me * circuits
    column = lax.broadcasted_iota(jnp.int32, shape, 1) + here * columns
    scale = jnp.where(row == column, 0.0, 1.0 / math.sqrt(rows * ORDER * amp))
    o_ref[0] = result[:, :columns] * scale
    o_ref[1] = result[:, half : half + columns] * scale

    for k in range(len(everyone)):
        slab(k).wait_send()


def fused(states, layer_angles, entangler, global_angles):
    circuits, _, local = states.shape
    rows = local // ORDER
    layers = layer_angles.shape[1]
    ens, amp = lax.axis_size("ens"), lax.axis_size("amp")
    total = ens * circuits
    share = rows // (2 * ens)
    depth = 2 * (share // 16) * 2 * ORDER
    _, angles, links = small_tables(layer_angles, entangler)
    return pl.pallas_call(
        functools.partial(fused_kernel, layers, ens, amp),
        out_shape=jax.ShapeDtypeStruct((2, circuits, total // amp), jnp.float32),
        in_specs=[pl.BlockSpec(memory_space=pl.ANY)] * 4,
        out_specs=pl.BlockSpec(memory_space=pltpu.VMEM),
        scratch_shapes=[
            pltpu.VMEM((1 + ens, 2 * ORDER, 2 * ORDER), jnp.bfloat16),
            pltpu.VMEM((1 + ens, 2 * ORDER, 2 * ORDER), jnp.bfloat16),
            pltpu.VMEM((2, 2 * ORDER, rows), jnp.bfloat16),
            pltpu.VMEM((circuits - 1, 2, local), jnp.bfloat16),
            pltpu.VMEM((circuits, rows, 2 * ORDER), jnp.bfloat16),
            pltpu.VMEM((ens, 2, ORDER * ORDER), jnp.bfloat16),
            pltpu.VMEM((ens, ORDER, 2 * ORDER), jnp.bfloat16),
            pltpu.VMEM((2, total, share, 2 * ORDER), jnp.bfloat16),
            pltpu.VMEM((ens, 8, ORDER), jnp.float32),
            pltpu.SMEM((ens, 8, ORDER), jnp.float32),
            pltpu.VMEM((total, 16, depth), jnp.bfloat16),
            pltpu.VMEM((2 * ens, 16, depth), jnp.bfloat16),
            pltpu.VMEM((total, ORDER), jnp.float32),
            pltpu.VMEM((ens * amp - 1, circuits, ORDER), jnp.float32),
            pltpu.VMEM((1, 2 * TABLE), jnp.float32),
            pltpu.SMEM((1, 2 * TABLE), jnp.float32),
            pltpu.SMEM(angles.shape, jnp.int32),
            pltpu.SMEM(links.shape, jnp.int32),
            pltpu.SMEM((2, circuits), jnp.int32),
            pltpu.VMEM(angles.shape, jnp.int32),
            pltpu.VMEM(links.shape, jnp.int32),
            pltpu.SemaphoreType.DMA((circuits,)),
            pltpu.SemaphoreType.DMA((6,)),
            pltpu.SemaphoreType.DMA((circuits, 2 * ens - 1)),
            pltpu.SemaphoreType.DMA((circuits, 2 * ens - 1)),
            pltpu.SemaphoreType.DMA((ens - 1,)),
            pltpu.SemaphoreType.DMA((ens - 1,)),
            pltpu.SemaphoreType.DMA((ens,)),
            pltpu.SemaphoreType.DMA((ens,)),
            pltpu.SemaphoreType.DMA((ens - 1,)),
            pltpu.SemaphoreType.DMA((ens - 1,)),
            pltpu.SemaphoreType.DMA((ens * amp - 1,)),
            pltpu.SemaphoreType.DMA((ens * amp - 1,)),
        ],
        compiler_params=pltpu.CompilerParams(
            vmem_limit_bytes=55208 << 10, collective_id=0, has_side_effects=True
        ),
    )(angles, links, jnp.transpose(global_angles), states)


def finish(summed, states, circuits):
    columns = lax.axis_size("ens") * circuits // lax.axis_size("amp")
    row_index = lax.axis_index("ens") * circuits + jnp.arange(circuits, dtype=jnp.int32)
    column_index = lax.axis_index("amp") * columns + jnp.arange(columns, dtype=jnp.int32)
    off_diagonal = jnp.where(row_index[:, None] == column_index[None, :], 0.0, 1.0).astype(jnp.float32)
    amplitudes = states.shape[2] * lax.axis_size("amp")
    return summed * (off_diagonal / math.sqrt(amplitudes))[None]


def fits(states, layers):
    circuits, _, local = states.shape
    ens, amp = lax.axis_size("ens"), lax.axis_size("amp")
    rows = local // ORDER
    return (
        rows == ens * ORDER and circuits % 8 == 0 and circuits <= 16 and layers == 16 and ens * circuits <= ORDER // 2
        and ens * circuits % amp == 0 and amp >= 2 and local <= 1 << 16 and ens > 1
    )


def scaled(coefficient, amplitudes):
    real_c = coefficient[0][:, None]
    imag_c = coefficient[1][:, None]
    return jnp.stack(
        [
            real_c * amplitudes[:, 0] - imag_c * amplitudes[:, 1],
            real_c * amplitudes[:, 1] + imag_c * amplitudes[:, 0],
        ],
        1,
    )


def choose_pair(upper_side, when_lower, when_upper):
    return (
        jnp.where(upper_side == 0, when_lower[0], when_upper[0]),
        jnp.where(upper_side == 0, when_lower[1], when_upper[1]),
    )


def pair_tile(mine, remote):
    products = jnp.einsum("ipa,jqa->pqij", mine, remote, preferred_element_type=jnp.float32)
    return jnp.stack([products[0, 0] + products[1, 1], products[0, 1] - products[1, 0]])


def body(states, layer_angles, entangler, global_angles):
    circuits = states.shape[0]
    if fits(states, layer_angles.shape[1]):
        return fused(states, layer_angles, entangler, global_angles)
    turned = all_layers(states, layer_angles, entangler).reshape(circuits, -1, 2, ORDER)
    current = jnp.swapaxes(turned, 1, 2).reshape(states.shape)
    swap_bit = lax.axis_size("amp").bit_length() - 2
    upper_side = lax.axis_index("amp") // 2**swap_bit % 2
    gate = rotation(global_angles[:, 0], global_angles[:, 1])
    partner = from_partner(current, "amp", swap_bit)
    coeff_self = choose_pair(upper_side, gate[0], gate[3])
    coeff_other = choose_pair(upper_side, gate[1], gate[2])
    final_states = (
        scaled(coeff_self, current.astype(jnp.float32))
        + scaled(coeff_other, partner.astype(jnp.float32))
    ).astype(jnp.bfloat16)
    partials = pair_tile(final_states, lax.all_gather(final_states, "ens", axis=0, tiled=True))
    summed = lax.psum_scatter(partials, "amp", scatter_dimension=2, tiled=True)
    return finish(summed, states, circuits)


def solution(mesh):
    return jax.shard_map(
        body,
        mesh=mesh,
        in_specs=(
            P(("groups", "ens"), None, "amp"),
            P(("groups", "ens"), None, None, None),
            P(("groups", "ens"), None, None),
            P(("groups", "ens"), None),
        ),
        out_specs=P(None, ("groups", "ens"), "amp"),
        check_vma=False,
    )
```

```python
import functools
import math

import jax
import jax.numpy as jnp
import numpy as np
from jax import lax
from jax.experimental import pallas as pl
from jax.experimental.pallas import tpu as pltpu
from jax.sharding import PartitionSpec as P

JOINED = 7
TABLE = 64
ORDER = 2**JOINED
LOW = 3
MESH_ID = pl.DeviceIdType.MESH


def from_partner(array, axis, bit):
    return lax.ppermute(array, axis, [(i, i ^ 1 << bit) for i in range(lax.axis_size(axis))])


def rotation(polar_index, azimuth_index):
    polar = polar_index.astype(jnp.float32) * (math.pi / TABLE)
    azimuth = azimuth_index.astype(jnp.float32) * (math.pi / TABLE)
    cos_polar = jnp.cos(polar)
    sin_polar = jnp.sin(polar)
    cos_azim = jnp.cos(azimuth)
    sin_azim = jnp.sin(azimuth)
    return (
        (cos_azim * cos_polar, -sin_azim * cos_polar),
        (-cos_azim * sin_polar, sin_azim * sin_polar),
        (cos_azim * sin_polar, sin_azim * sin_polar),
        (cos_azim * cos_polar, sin_azim * cos_polar),
    )


def bit_of(shape, dim, bit, shift=0):
    return (lax.broadcasted_iota(jnp.int32, shape, dim) >> (bit - shift)) & 1


class Indexed:
    def __init__(self, circuits, circuit, table_ref, angle_ref, link_ref):
        self.circuits, self.circuit = circuits, circuit
        self.table, self.angle, self.link = table_ref, angle_ref, link_ref

    def cos_sin(self, layer, k, which):
        index = self.angle[(self.circuit * JOINED + k) * 2 + which, layer]
        return self.table[0, index], self.table[0, index + TABLE]

    def flip(self, layer, k):
        return 1.0 - 2.0 * self.link[k * self.circuits + self.circuit, layer].astype(jnp.float32)


class Listed:
    def __init__(self, ref):
        self.ref = ref

    def entry(self, r, layer):
        return self.ref[r // 8, r % 8 * 16 + layer]

    def cos_sin(self, layer, k, which):
        return self.entry(2 * k + which, layer), self.entry(2 * JOINED + 2 * k + which, layer)

    def flip(self, layer, k):
        return self.entry(4 * JOINED + k, layer)


def part_factor(tables, layer, upper, high):
    qubits = range(LOW, JOINED) if high else range(LOW)
    shape = (2 ** len(qubits), ORDER)
    shift = LOW if high else 0
    row = {k: bit_of(shape, 0, k, shift) for k in qubits}
    lane = {k: bit_of(shape, 1, k) for k in range(JOINED)}
    out = row if upper else lane
    real = imag = None
    turn = None
    for k in qubits:
        cos_t, sin_t = tables.cos_sin(layer, k, 0)
        cos_f, sin_f = tables.cos_sin(layer, k, 1)
        side = (2 * out[k] - 1).astype(jnp.float32)
        factor = jnp.where(row[k] == lane[k], cos_t, side * sin_t)
        turn = factor if turn is None else turn * factor
        step = side * sin_f
        if real is None:
            real, imag = jnp.full(shape, cos_f), step
        else:
            real, imag = real * cos_f - imag * step, real * step + imag * cos_f
    for k in range(JOINED - 1):
        inside = k in qubits and k + 1 in qubits
        if inside or (not upper and not high and k == LOW - 1):
            turn = jnp.where(out[k] * out[k + 1] == 1, tables.flip(layer, k) * turn, turn)
    return real * turn, imag * turn


def build(tables, layer, upper, w_ref):
    low_real, low_imag = part_factor(tables, layer, upper, False)
    high_real, high_imag = part_factor(tables, layer, upper, True)
    lows = [(low_real, low_imag)] * 2
    if upper:
        crossed = bit_of(low_real.shape, 0, LOW - 1) == 1
        flip = tables.flip(layer, LOW - 1)
        lows[1] = tuple(jnp.where(crossed, flip * v, v) for v in lows[0])
    for pair in range(ORDER // 16):
        reals, imags = [], []
        for odd in range(2):
            r = 2 * pair + odd
            a_real = jnp.broadcast_to(high_real[r : r + 1], (8, ORDER))
            a_imag = jnp.broadcast_to(high_imag[r : r + 1], (8, ORDER))
            b_real, b_imag = lows[odd]
            reals.append(a_real * b_real - a_imag * b_imag)
            imags.append(a_real * b_imag + a_imag * b_real)
        real = jnp.concatenate(reals, 0)
        imag = jnp.concatenate(imags, 0)
        plus, minus = imag.astype(jnp.bfloat16), (-imag).astype(jnp.bfloat16)
        real = real.astype(jnp.bfloat16)
        top, bottom = (minus, plus) if upper else (plus, minus)
        rows = pl.ds(16 * pair, 16)
        rows_below = pl.ds(ORDER + 16 * pair, 16)
        w_ref[rows, :ORDER] = real
        w_ref[rows, ORDER:] = top
        w_ref[rows_below, :ORDER] = bottom
        w_ref[rows_below, ORDER:] = real


def bridge(values):
    rows, columns = values.shape
    shape = (1, 8, columns)
    odd = bit_of(shape, 1, 0) * bit_of(shape, 2, JOINED - 1)
    sign = (1 - 2 * odd).astype(jnp.float32)
    return (values.reshape(rows // 8, 8, columns) * sign).reshape(rows, columns)


def spread(x_ref, t_ref):
    def some(step, carry):
        flat = x_ref[:, pl.ds(pl.multiple_of(step * 16 * ORDER, 16 * ORDER), 16 * ORDER)]
        tiles = flat.astype(jnp.float32).reshape(2, 16, ORDER).astype(jnp.bfloat16)
        rows_at = pl.ds(pl.multiple_of(step * 16, 16), 16)
        t_ref[rows_at, :ORDER] = tiles[0]
        t_ref[rows_at, ORDER:] = tiles[1]
        return carry

    lax.fori_loop(0, t_ref.shape[0] // 16, some, 0, unroll=4)


def run_layers(layers, chains):
    for tables, _, wl_ref, _, _ in chains:
        build(tables, 0, False, wl_ref)

    def two(pair, carry):
        layer = 2 * pair
        following = jnp.minimum(layer + 2, layers - 2)
        for tables, t_ref, wl_ref, wu_ref, s_ref in chains:
            y = jnp.dot(t_ref[...], wl_ref[...], preferred_element_type=jnp.float32)
            y = bridge(y).astype(jnp.bfloat16)
            for b in range(t_ref.shape[0] // ORDER):
                for p in range(2):
                    s_ref[p * ORDER : (p + 1) * ORDER, b * ORDER : (b + 1) * ORDER] = y[
                        b * ORDER : (b + 1) * ORDER, p * ORDER : (p + 1) * ORDER
                    ]
            build(tables, layer + 1, True, wu_ref)
        for tables, t_ref, wl_ref, wu_ref, s_ref in chains:
            y = jnp.dot(wu_ref[...], s_ref[...], preferred_element_type=jnp.float32)
            y = bridge(y).astype(jnp.bfloat16)
            for b in range(t_ref.shape[0] // ORDER):
                for p in range(2):
                    t_ref[b * ORDER : (b + 1) * ORDER, p * ORDER : (p + 1) * ORDER] = y[
                        p * ORDER : (p + 1) * ORDER, b * ORDER : (b + 1) * ORDER
                    ]
            build(tables, following, False, wl_ref)
        return carry

    lax.fori_loop(0, layers // 2, two, 0)


def layers_kernel(circuits, layers, table_ref, angle_ref, link_ref, x_ref, t_ref, wl_ref, wu_ref, s_ref):
    tables = Indexed(circuits, pl.program_id(0), table_ref, angle_ref, link_ref)
    spread(x_ref.at[0], t_ref.at[0])
    run_layers(layers, [(tables, t_ref.at[0], wl_ref, wu_ref, s_ref)])


def small_tables(layer_angles, entangler):
    circuits, layers = layer_angles.shape[:2]
    angle = np.arange(TABLE, dtype=np.float64) * (math.pi / TABLE)
    table = jnp.asarray(np.concatenate([np.cos(angle), np.sin(angle)]).astype(np.float32))[None]
    angles = jnp.transpose(layer_angles, (0, 2, 3, 1)).reshape(circuits * JOINED * 2, layers)
    links = jnp.transpose(entangler, (2, 0, 1)).reshape((JOINED - 1) * circuits, layers)
    return table, angles, links


def all_layers(states, layer_angles, entangler):
    circuits, _, local = states.shape
    rows = local // ORDER
    layers = layer_angles.shape[1]
    smem = pl.BlockSpec(memory_space=pltpu.SMEM)
    return pl.pallas_call(
        functools.partial(layers_kernel, circuits, layers),
        grid=(circuits,),
        out_shape=jax.ShapeDtypeStruct((circuits, rows, 2 * ORDER), jnp.bfloat16),
        in_specs=[smem, smem, smem, pl.BlockSpec((1, 2, local), lambda g: (g, 0, 0))],
        out_specs=pl.BlockSpec((1, rows, 2 * ORDER), lambda g: (g, 0, 0)),
        scratch_shapes=[
            pltpu.VMEM((2 * ORDER, 2 * ORDER), jnp.bfloat16),
            pltpu.VMEM((2 * ORDER, 2 * ORDER), jnp.bfloat16),
            pltpu.VMEM((2 * ORDER, rows), jnp.bfloat16),
        ],
        compiler_params=pltpu.CompilerParams(vmem_limit_bytes=32 << 20),
    )(*small_tables(layer_angles, entangler), states)


def gate_pair(gate, low, high):
    outs = []
    for r in range(2):
        a_real, a_imag, b_real, b_imag = (gate[4 * r + k] for k in range(4))
        real = a_real * low[0] - a_imag * low[1] + (b_real * high[0] - b_imag * high[1])
        imag = a_real * low[1] + a_imag * low[0] + (b_real * high[1] + b_imag * high[0])
        outs.append((real, imag))
    return outs


def exact_dot(values, picks, dims):
    total = None
    for _ in range(3):
        term = values.astype(jnp.bfloat16)
        values = values - term.astype(jnp.float32)
        operands = (term, picks) if dims[0] == "values" else (picks, term)
        part = lax.dot_general(*operands, (dims[1], ((), ())), preferred_element_type=jnp.float32)
        total = part if total is None else total + part
    return total


def listed(angles, links):
    angle = angles.astype(jnp.float32) * (math.pi / TABLE)
    layers = angle.shape[1]
    flips = 1.0 - 2.0 * links.astype(jnp.float32)
    unused = jnp.zeros((64 - 4 * JOINED - (JOINED - 1), layers), jnp.float32)
    values = jnp.concatenate([jnp.cos(angle), jnp.sin(angle), flips, unused], 0)
    shape = (layers, ORDER)
    source = lax.broadcasted_iota(jnp.int32, shape, 0)
    again = jnp.where(source == lax.broadcasted_iota(jnp.int32, shape, 1) % layers, 1.0, 0.0).astype(jnp.bfloat16)
    repeated = exact_dot(values, again, ("values", ((1,), (0,)))).reshape(8, 8, ORDER)
    shape = (1, 8, ORDER)
    mine = lax.broadcasted_iota(jnp.int32, shape, 1) == lax.broadcasted_iota(jnp.int32, shape, 2) // layers
    return jnp.where(mine, repeated, 0.0).sum(1)


GATE_ROW = 7


def two_terms(values):
    first = values.astype(jnp.bfloat16)
    return jnp.concatenate([first, (values - first.astype(jnp.float32)).astype(jnp.bfloat16)], 0)


def fused_kernel(
    layers, ens, amp,
    angle_hbm, link_hbm, global_hbm, x_hbm, o_ref,
    wl_ref, wu_ref, s_ref, x_ref, t_ref, first_x, first_t, r_ref, c_ref, cs_ref, f_ref, h_ref, l_ref, m_ref, p_ref, q_ref,
    table_vmem, table_ref, angle_ref, link_ref, global_ref, angle_vmem, link_vmem,
    load_sem, small_sem, send_sem, recv_sem, first_send, first_recv, half_send, half_recv,
    gate_send, gate_recv, sum_send, sum_recv,
):
    circuits, rows, _ = t_ref.shape
    total = ens * circuits
    share = rows // (2 * ens)
    parts = share // 16
    half = 2 * ORDER // 4
    bit = amp.bit_length() - 2
    me = lax.axis_index("ens")
    here = lax.axis_index("amp")
    side = (here // 2**bit) % 2
    rest = here - side * 2**bit
    square = ORDER * ORDER

    barrier = pltpu.get_barrier_semaphore()
    everyone = [(k // amp, k % amp) for k in range(1, ens * amp)]
    everyone = sorted(everyone, key=lambda p: (abs(2 * p[0] - ens), -p[1]))
    near = [(e, a) for e, a in everyone if a % 2 == 0]
    for e, a in near:
        pl.semaphore_signal(
            barrier, inc=1, device_id={"ens": (me + e) % ens, "amp": (here + a) % amp}, device_id_type=MESH_ID
        )
    mate = here + 1 - 2 * (here % 2)
    pl.semaphore_signal(barrier, inc=1, device_id={"amp": mate}, device_id_type=MESH_ID)

    def load(circuit):
        return pltpu.make_async_copy(x_hbm.at[circuit], x_ref.at[circuit - 1], load_sem.at[circuit])

    def block(index):
        return x_hbm.at[0, :, pl.ds(pl.multiple_of(index * square, square), square)]

    own_block = pltpu.make_async_copy(block(me), first_x.at[me], load_sem.at[0])
    smalls = [
        pltpu.make_async_copy(source, target, small_sem.at[i])
        for i, (source, target) in enumerate(
            (
                (table_vmem, table_ref), (angle_hbm, angle_ref), (link_hbm, link_ref), (global_hbm, global_ref),
                (angle_hbm, angle_vmem), (link_hbm, link_vmem),
            )
        )
    ]
    for copy in smalls[1:]:
        copy.start()
    for circuit in range(1, circuits):
        load(circuit).start()
    own_block.start()

    def first_block(k, source):
        to = (me + k) % ens
        return pltpu.make_async_remote_copy(
            src_ref=block(to),
            dst_ref=first_x.at[source],
            send_sem=first_send.at[k - 1],
            recv_sem=first_recv.at[k - 1],
            device_id={"ens": to},
            device_id_type=MESH_ID,
        )

    far_first = sorted(range(1, ens), key=lambda k: abs(2 * k - ens))
    entry = lax.broadcasted_iota(jnp.int32, table_vmem.shape, 1)
    angle = (entry % TABLE).astype(jnp.float32) * (math.pi / TABLE)
    table_vmem[...] = jnp.where(entry < TABLE, jnp.cos(angle), jnp.sin(angle))
    smalls[0].start()
    pl.semaphore_wait(barrier, len(near) + 1)
    for k in far_first:
        first_block(k, me).start()

    for copy in smalls:
        copy.wait()
    links = jnp.concatenate([link_vmem[k * circuits : k * circuits + 1] for k in range(JOINED - 1)], 0)
    tile = listed(angle_vmem[: 2 * JOINED], links)
    lane = lax.broadcasted_iota(jnp.int32, (1, ORDER), 1)
    line = jnp.zeros((1, ORDER), jnp.float32)
    for circuit in range(circuits):
        polar, azimuth = global_ref[0, circuit], global_ref[1, circuit]
        cos_t, sin_t = table_ref[0, polar], table_ref[0, polar + TABLE]
        cos_f, sin_f = table_ref[0, azimuth], table_ref[0, azimuth + TABLE]
        entries = (
            cos_f * cos_t, -sin_f * cos_t, -cos_f * sin_t, sin_f * sin_t,
            cos_f * sin_t, sin_f * sin_t, cos_f * cos_t, sin_f * cos_t,
        )
        for k, entry in enumerate(entries):
            line = jnp.where(lane == circuit * 8 + k, entry, line)
    is_gate = lax.broadcasted_iota(jnp.int32, (8, ORDER), 0) == GATE_ROW
    c_ref[pl.ds(me, 1)] = jnp.where(is_gate, line, tile)[None]

    def gate_copy(k, source):
        return pltpu.make_async_remote_copy(
            src_ref=c_ref.at[source],
            dst_ref=c_ref.at[source],
            send_sem=gate_send.at[k - 1],
            recv_sem=gate_recv.at[k - 1],
            device_id={"ens": (me + k) % ens},
            device_id_type=MESH_ID,
        )

    for k in far_first:
        gate_copy(k, me).start()

    peers = sorted(((k // ens, k % ens) for k in range(1, 2 * ens)), key=lambda p: (abs(2 * p[1] - ens), p[0]))

    def piece(k, circuit, from_side, from_ens):
        across, along = peers[k]
        to_side = side + across - 2 * side * across
        to_ens = (me + along) % ens
        start = pl.multiple_of((2 * to_ens + to_side) * share, share)
        return pltpu.make_async_remote_copy(
            src_ref=t_ref.at[circuit, pl.ds(start, share)],
            dst_ref=r_ref.at[from_side, from_ens * circuits + circuit],
            send_sem=send_sem.at[circuit, k],
            recv_sem=recv_sem.at[circuit, k],
            device_id={"ens": to_ens, "amp": to_side * 2**bit + rest},
            device_id_type=MESH_ID,
        )

    def half_copy(e, from_side):
        to_side = 1 - side
        return pltpu.make_async_remote_copy(
            src_ref=first_t.at[e, pl.ds(pl.multiple_of(to_side * share, share), share)],
            dst_ref=r_ref.at[from_side, e * circuits],
            send_sem=half_send.at[e],
            recv_sem=half_recv.at[e],
            device_id={"amp": to_side * 2**bit + rest},
            device_id_type=MESH_ID,
        )

    def chain(circuit, i):
        load(circuit).wait()
        spread(x_ref.at[circuit - 1], t_ref.at[circuit])
        tables = Indexed(circuits, circuit, table_ref, angle_ref, link_ref)
        return tables, t_ref.at[circuit], wl_ref.at[i], wu_ref.at[i], s_ref.at[i]

    def send(circuit):
        for k in range(len(peers)):
            piece(k, circuit, side, me).start()
        own = pl.multiple_of((2 * me + side) * share, share)
        r_ref[side, me * circuits + circuit] = t_ref[circuit, pl.ds(own, share), :]

    def compute(pair, carry):
        both = (2 * pair + 1, 2 * pair + 2)
        run_layers(layers, [chain(circuit, i) for i, circuit in enumerate(both)])
        for circuit in both:
            send(circuit)
        return carry

    lax.fori_loop(0, circuits // 2 - 1, compute, 0)

    for k in range(1, ens):
        gate_copy(k, (me + ens - k) % ens).wait_recv()
    scalars = pltpu.make_async_copy(c_ref, cs_ref, small_sem.at[0])
    scalars.start()
    own_block.wait()
    for k in range(1, ens):
        first_block(k, (me + ens - k) % ens).wait_recv()
    for e in range(ens):
        spread(first_x.at[e], first_t.at[e])
    scalars.wait()
    last = circuits - 1
    run_layers(
        layers,
        [chain(last, 0)]
        + [
            (
                Listed(cs_ref.at[e]), first_t.at[e], wl_ref.at[1 + e], wu_ref.at[1 + e],
                s_ref.at[1, :, e * ORDER : (e + 1) * ORDER],
            )
            for e in range(ens)
        ],
    )
    send(last)
    for e in range(ens):
        half_copy(e, side).start()
        r_ref[side, e * circuits] = first_t[e, pl.ds(pl.multiple_of(side * share, share), share), :]

    f_ref[...] = jnp.zeros_like(f_ref)
    l_ref[...] = jnp.zeros_like(l_ref)

    depth = f_ref.shape[2]

    def gram(circuit, carry):
        @pl.when(circuit == 0)
        def _():
            for e in range(ens):
                half_copy(e, 1 - side).wait_recv()

        @pl.when(circuit != 0)
        def _():
            for k, (across, along) in enumerate(peers):
                piece(k, circuit, side + across - 2 * side * across, (me + ens - along) % ens).wait_recv()

        for e in range(ens):
            which = e * circuits + circuit
            gate = [cs_ref[e, GATE_ROW, circuit * 8 + k] for k in range(8)]
            low = r_ref[0, which].astype(jnp.float32)
            high = r_ref[1, which].astype(jnp.float32)
            outs = gate_pair(gate, (low[:, :ORDER], low[:, ORDER:]), (high[:, :ORDER], high[:, ORDER:]))
            for x, (real, imag) in enumerate(outs):
                real = real.astype(jnp.bfloat16)
                imag = imag.astype(jnp.bfloat16)
                minus = -real
                for part in range(parts):
                    at = (x * parts + part) * 2 * ORDER
                    take = slice(16 * part, 16 * part + 16)
                    for ref, row in ((f_ref, which), (h_ref, e)):
                        ref[row, :, at : at + ORDER] = real[take]
                        ref[row, :, at + ORDER : at + 2 * ORDER] = imag[take]
                    h_ref[ens + e, :, at : at + ORDER] = imag[take]
                    h_ref[ens + e, :, at + ORDER : at + 2 * ORDER] = minus[take]
        fresh = 2 * ens * 16
        full = lax.dot_general(
            f_ref[...].reshape(total * 16, depth), h_ref[...].reshape(fresh, depth),
            (((1,), (1,)), ((), ())), preferred_element_type=jnp.float32,
        )
        shape = (1, 16, fresh)
        same = lax.broadcasted_iota(jnp.int32, shape, 1) == lax.broadcasted_iota(jnp.int32, shape, 2) % 16
        kept = jnp.where(same, full.reshape(total, 16, fresh), 0.0).sum(1)

        shape = (fresh, ORDER)
        source = lax.broadcasted_iota(jnp.int32, shape, 0) // 16
        target = lax.broadcasted_iota(jnp.int32, shape, 1)
        place = jnp.where(source >= ens, half + (source - ens) * circuits, source * circuits) + circuit
        picks = jnp.where(place == target, 1.0, 0.0).astype(jnp.bfloat16)
        above = jnp.dot(two_terms(kept), picks, preferred_element_type=jnp.float32)

        shape = (half, fresh)
        row = lax.broadcasted_iota(jnp.int32, shape, 0)
        is_imag = lax.broadcasted_iota(jnp.int32, shape, 1) // 16 >= ens
        before = (row % circuits < circuit) & (row < total)
        doubled = kept if total == half else jnp.concatenate([kept, jnp.zeros((half - total, fresh), jnp.float32)], 0)
        stacked = jnp.concatenate(
            [jnp.where(before & ~is_imag, doubled, 0.0), jnp.where(before & is_imag, -doubled, 0.0)], 0
        )
        shape = (total, fresh)
        row = lax.broadcasted_iota(jnp.int32, shape, 0)
        source = lax.broadcasted_iota(jnp.int32, shape, 1) // 16 % ens
        gather = jnp.where(row == source * circuits + circuit, 1.0, 0.0).astype(jnp.bfloat16)
        mirrored = lax.dot_general(
            gather, two_terms(stacked), (((1,), (1,)), ((), ())), preferred_element_type=jnp.float32
        )
        l_ref[...] += above[:total] + above[total:] + (mirrored[:, :ORDER] + mirrored[:, ORDER:])
        return carry

    lax.fori_loop(0, circuits, gram, 0)

    mate_sum = pltpu.make_async_remote_copy(
        src_ref=l_ref, dst_ref=m_ref, send_sem=sum_send.at[len(near)], recv_sem=sum_recv.at[len(near)],
        device_id={"amp": mate}, device_id_type=MESH_ID,
    )
    mate_sum.start()
    mate_sum.wait_recv()
    p_ref[...] = l_ref[...] + m_ref[...]

    def slab(k):
        e, a = near[k]
        to = (me + e) % ens
        return pltpu.make_async_remote_copy(
            src_ref=p_ref.at[pl.ds(pl.multiple_of(to * circuits, circuits), circuits)],
            dst_ref=q_ref.at[k],
            send_sem=sum_send.at[k],
            recv_sem=sum_recv.at[k],
            device_id={"ens": to, "amp": (here + a) % amp},
            device_id_type=MESH_ID,
        )

    for k in range(len(near)):
        slab(k).start()
    for k in range(1, ens):
        gate_copy(k, me).wait_send()
        first_block(k, me).wait_send()
    for e in range(ens):
        half_copy(e, side).wait_send()

    def drain(circuit, carry):
        for k in range(len(peers)):
            piece(k, circuit, side, me).wait_send()
        return carry

    lax.fori_loop(1, circuits, drain, 0)

    result = p_ref[pl.ds(pl.multiple_of(me * circuits, circuits), circuits)]
    for k in range(len(near)):
        slab(k).wait_recv()
        result = result + q_ref[k]
    columns = total // amp
    result = pltpu.roll(result, (2 * half - here * columns) % (2 * half), 1)
    shape = (circuits, columns)
    row = lax.broadcasted_iota(jnp.int32, shape, 0) + me * circuits
    column = lax.broadcasted_iota(jnp.int32, shape, 1) + here * columns
    scale = jnp.where(row == column, 0.0, 1.0 / math.sqrt(rows * ORDER * amp))
    o_ref[0] = result[:, :columns] * scale
    o_ref[1] = result[:, half : half + columns] * scale

    for k in range(len(near)):
        slab(k).wait_send()
    mate_sum.wait_send()


def fused(states, layer_angles, entangler, global_angles):
    circuits, _, local = states.shape
    rows = local // ORDER
    layers = layer_angles.shape[1]
    ens, amp = lax.axis_size("ens"), lax.axis_size("amp")
    total = ens * circuits
    share = rows // (2 * ens)
    depth = 2 * (share // 16) * 2 * ORDER
    _, angles, links = small_tables(layer_angles, entangler)
    return pl.pallas_call(
        functools.partial(fused_kernel, layers, ens, amp),
        out_shape=jax.ShapeDtypeStruct((2, circuits, total // amp), jnp.float32),
        in_specs=[pl.BlockSpec(memory_space=pl.ANY)] * 4,
        out_specs=pl.BlockSpec(memory_space=pltpu.VMEM),
        scratch_shapes=[
            pltpu.VMEM((1 + ens, 2 * ORDER, 2 * ORDER), jnp.bfloat16),
            pltpu.VMEM((1 + ens, 2 * ORDER, 2 * ORDER), jnp.bfloat16),
            pltpu.VMEM((2, 2 * ORDER, rows), jnp.bfloat16),
            pltpu.VMEM((circuits - 1, 2, local), jnp.bfloat16),
            pltpu.VMEM((circuits, rows, 2 * ORDER), jnp.bfloat16),
            pltpu.VMEM((ens, 2, ORDER * ORDER), jnp.bfloat16),
            pltpu.VMEM((ens, ORDER, 2 * ORDER), jnp.bfloat16),
            pltpu.VMEM((2, total, share, 2 * ORDER), jnp.bfloat16),
            pltpu.VMEM((ens, 8, ORDER), jnp.float32),
            pltpu.SMEM((ens, 8, ORDER), jnp.float32),
            pltpu.VMEM((total, 16, depth), jnp.bfloat16),
            pltpu.VMEM((2 * ens, 16, depth), jnp.bfloat16),
            pltpu.VMEM((total, ORDER), jnp.float32),
            pltpu.VMEM((total, ORDER), jnp.float32),
            pltpu.VMEM((total, ORDER), jnp.float32),
            pltpu.VMEM((ens * amp // 2 - 1, circuits, ORDER), jnp.float32),
            pltpu.VMEM((1, 2 * TABLE), jnp.float32),
            pltpu.SMEM((1, 2 * TABLE), jnp.float32),
            pltpu.SMEM(angles.shape, jnp.int32),
            pltpu.SMEM(links.shape, jnp.int32),
            pltpu.SMEM((2, circuits), jnp.int32),
            pltpu.VMEM(angles.shape, jnp.int32),
            pltpu.VMEM(links.shape, jnp.int32),
            pltpu.SemaphoreType.DMA((circuits,)),
            pltpu.SemaphoreType.DMA((6,)),
            pltpu.SemaphoreType.DMA((circuits, 2 * ens - 1)),
            pltpu.SemaphoreType.DMA((circuits, 2 * ens - 1)),
            pltpu.SemaphoreType.DMA((ens - 1,)),
            pltpu.SemaphoreType.DMA((ens - 1,)),
            pltpu.SemaphoreType.DMA((ens,)),
            pltpu.SemaphoreType.DMA((ens,)),
            pltpu.SemaphoreType.DMA((ens - 1,)),
            pltpu.SemaphoreType.DMA((ens - 1,)),
            pltpu.SemaphoreType.DMA((ens * amp // 2,)),
            pltpu.SemaphoreType.DMA((ens * amp // 2,)),
        ],
        compiler_params=pltpu.CompilerParams(
            vmem_limit_bytes=55208 << 10, collective_id=0, has_side_effects=True
        ),
    )(angles, links, jnp.transpose(global_angles), states)


def finish(summed, states, circuits):
    columns = lax.axis_size("ens") * circuits // lax.axis_size("amp")
    row_index = lax.axis_index("ens") * circuits + jnp.arange(circuits, dtype=jnp.int32)
    column_index = lax.axis_index("amp") * columns + jnp.arange(columns, dtype=jnp.int32)
    off_diagonal = jnp.where(row_index[:, None] == column_index[None, :], 0.0, 1.0).astype(jnp.float32)
    amplitudes = states.shape[2] * lax.axis_size("amp")
    return summed * (off_diagonal / math.sqrt(amplitudes))[None]


def fits(states, layers):
    circuits, _, local = states.shape
    ens, amp = lax.axis_size("ens"), lax.axis_size("amp")
    rows = local // ORDER
    return (
        rows == ens * ORDER and circuits % 8 == 0 and circuits <= 16 and layers == 16 and ens * circuits <= ORDER // 2
        and ens * circuits % amp == 0 and amp >= 2 and local <= 1 << 16 and ens > 1
    )


def scaled(coefficient, amplitudes):
    real_c = coefficient[0][:, None]
    imag_c = coefficient[1][:, None]
    return jnp.stack(
        [
            real_c * amplitudes[:, 0] - imag_c * amplitudes[:, 1],
            real_c * amplitudes[:, 1] + imag_c * amplitudes[:, 0],
        ],
        1,
    )


def choose_pair(upper_side, when_lower, when_upper):
    return (
        jnp.where(upper_side == 0, when_lower[0], when_upper[0]),
        jnp.where(upper_side == 0, when_lower[1], when_upper[1]),
    )


def pair_tile(mine, remote):
    products = jnp.einsum("ipa,jqa->pqij", mine, remote, preferred_element_type=jnp.float32)
    return jnp.stack([products[0, 0] + products[1, 1], products[0, 1] - products[1, 0]])


def body(states, layer_angles, entangler, global_angles):
    circuits = states.shape[0]
    if fits(states, layer_angles.shape[1]):
        return fused(states, layer_angles, entangler, global_angles)
    turned = all_layers(states, layer_angles, entangler).reshape(circuits, -1, 2, ORDER)
    current = jnp.swapaxes(turned, 1, 2).reshape(states.shape)
    swap_bit = lax.axis_size("amp").bit_length() - 2
    upper_side = lax.axis_index("amp") // 2**swap_bit % 2
    gate = rotation(global_angles[:, 0], global_angles[:, 1])
    partner = from_partner(current, "amp", swap_bit)
    coeff_self = choose_pair(upper_side, gate[0], gate[3])
    coeff_other = choose_pair(upper_side, gate[1], gate[2])
    final_states = (
        scaled(coeff_self, current.astype(jnp.float32))
        + scaled(coeff_other, partner.astype(jnp.float32))
    ).astype(jnp.bfloat16)
    partials = pair_tile(final_states, lax.all_gather(final_states, "ens", axis=0, tiled=True))
    summed = lax.psum_scatter(partials, "amp", scatter_dimension=2, tiled=True)
    return finish(summed, states, circuits)


def solution(mesh):
    return jax.shard_map(
        body,
        mesh=mesh,
        in_specs=(
            P(("groups", "ens"), None, "amp"),
            P(("groups", "ens"), None, None, None),
            P(("groups", "ens"), None, None),
            P(("groups", "ens"), None),
        ),
        out_specs=P(None, ("groups", "ens"), "amp"),
        check_vma=False,
    )
```
